32 devices in a mesh: lon: 4 (over y, x), lat: 8 (over z, core).
Axes of the slice: x: 2, y: 2, z: 4, core: 2. Of those that a mesh axis runs over, the one named last changes fastest.
Arguments:
- ocean_field: bfloat16 [256, 1024, 128], P('lon', 'lat'), may hold values from -6 to 6
- wet_tiles: int32 [4, 16], P('lon', 'lat'), may hold values from 0 to 1
- conv_weight: bfloat16 [2, 7, 7, 128], replicated, may hold values from -0.875 to 0.875
- norm_gain: float32 [2, 128], replicated, may hold values from 0.1 to 1.9
- norm_bias: float32 [2, 128], replicated, may hold values from -3 to 3
- inner_weight: bfloat16 [2, 128, 256], replicated, may hold values from -0.5 to 0.5
- inner_bias: float32 [2, 256], replicated, may hold values from -3 to 3
- outer_weight: bfloat16 [2, 256, 128], replicated, may hold values from -0.375 to 0.375
- outer_bias: float32 [2, 128], replicated, may hold values from -3 to 3
Outputs:
- updated_field: bfloat16 [256, 1024, 128], P('lon', 'lat')
The draws below stay inside these ranges and needn't reach their ends.
All inputs are finite; a program needn't handle non-finite values.
Results may differ from the reference program's by a relative error of at most 0.0069.
Values may be sent and summed in bfloat16 or wider, within the bound.
No kernel may reach another device: no remote copies, remote signals or barrier semaphores. Data moves between devices by JAX's collectives and lax.ppermute only.
A program may use at most 64 MiB of HBM per device.

```python
import jax
import jax.numpy as jnp
from jax import lax

C = 128
HID = 256
KSIZE = 7
TILE = 64
LAYERS = 2
TLON = 1
TLAT = 2
GLON = 4
GLAT = 16
NLON = 256
NLAT = 1024


def draw_wet_tiles(key, part):
    band_key, roll_key = jax.random.split(jax.random.fold_in(key, 7))
    blocks_lon = GLON // TLON
    blocks_lat = GLAT // TLAT
    wet_level = jax.random.randint(band_key, (blocks_lon, blocks_lat), 0, 3)
    northern = (jnp.arange(blocks_lat, dtype=jnp.int32) >= blocks_lat // 2).astype(jnp.int32)
    wet_level = wet_level + northern[None, :]
    level_tiles = jnp.repeat(jnp.repeat(wet_level, TLON, axis=0), TLAT, axis=1)
    rolled = jax.random.randint(roll_key, (GLON, GLAT), 0, 8)
    return (rolled < jnp.left_shift(jnp.int32(1), level_tiles)).astype(jnp.int32)


def levels(rng, extent, shards, least, largest):
    level, own = 1.0, jax.random.fold_in(rng, 6)
    for position, parts in shards:
        heights = jnp.exp(jax.random.uniform(jax.random.fold_in(own, position), (parts,), jnp.float32, least / len(shards), largest / len(shards)))
        level = level * jnp.repeat(heights, extent[position] // parts).reshape([-1 if axis == position else 1 for axis in range(len(extent))])
    return level


def gaussian(stream_key, extent, spread, most, pieces=(), kind=jnp.bfloat16):
    array = jax.random.normal(stream_key, extent, jnp.float32) * spread
    if len(pieces) > 0:
        array = levels(stream_key, extent, pieces, -0.22, 0.18) * array
    return jnp.clip(array, min=-most, max=most).astype(kind)


def setup_inputs(seed: int = 0) -> dict:
    seeds = jax.random.split(jax.random.key(seed), 10)
    ocean_field = gaussian(seeds[0], (NLON, NLAT, C), 1.0, 6.0, ((0, 4), (1, 8)))
    wet_tiles = draw_wet_tiles(jax.random.fold_in(seeds[9], 71), 0)
    conv_weight = gaussian(seeds[2], (LAYERS, KSIZE, KSIZE, C), (KSIZE * KSIZE) ** -0.5, 0.875)
    norm_gain = jnp.clip(1.0 + 0.18 * jax.random.normal(seeds[3], (LAYERS, C), jnp.float32), 0.1, 1.9)
    norm_bias = gaussian(seeds[4], (LAYERS, C), 0.5, 3.0, (), jnp.float32)
    inner_weight = gaussian(seeds[5], (LAYERS, C, HID), C ** -0.5, 0.5)
    inner_bias = gaussian(seeds[6], (LAYERS, HID), 0.5, 3.0, (), jnp.float32)
    outer_weight = gaussian(seeds[7], (LAYERS, HID, C), HID ** -0.5, 0.375)
    outer_bias = gaussian(seeds[8], (LAYERS, C), 0.5, 3.0, (), jnp.float32)
    return dict(ocean_field=ocean_field, wet_tiles=wet_tiles, conv_weight=conv_weight, norm_gain=norm_gain, norm_bias=norm_bias, inner_weight=inner_weight, inner_bias=inner_bias, outer_weight=outer_weight, outer_bias=outer_bias)


def mix_rows(rows, gain, bias, inner_weight, inner_bias, outer_weight, outer_bias):
    values = rows.astype(jnp.float32)
    row_mean = lax.optimization_barrier(jnp.mean(values, axis=-1, keepdims=True))
    centered = values - row_mean
    variance = lax.optimization_barrier(jnp.mean(centered * centered, axis=-1, keepdims=True))
    normed = (centered * lax.rsqrt(variance + 1e-06) * gain + bias).astype(jnp.bfloat16)
    hidden = jax.nn.gelu(jnp.dot(normed, inner_weight, preferred_element_type=jnp.float32) + inner_bias, approximate=False).astype(jnp.bfloat16)
    return (jnp.dot(hidden, outer_weight, preferred_element_type=jnp.float32) + outer_bias).astype(jnp.bfloat16)

def depthwise(padded, weights, rows, cols):
    total = jnp.zeros((rows, cols, padded.shape[2]), jnp.float32)
    for shift_a in range(7):
        for shift_b in range(7):
            total = total + padded[shift_a:shift_a + rows, shift_b:shift_b + cols].astype(jnp.float32) * weights[shift_a, shift_b].astype(jnp.float32)
    return total.astype(jnp.bfloat16)

def reference(ocean_field, wet_tiles, conv_weight, norm_gain, norm_bias, inner_weight, inner_bias, outer_weight, outer_bias):
    cell_wet = jnp.repeat(jnp.repeat(wet_tiles, TILE, axis=0), TILE, axis=1)[:, :, None] > 0
    current = jnp.where(cell_wet, ocean_field, jnp.zeros((), ocean_field.dtype))
    for layer in range(LAYERS):
        padded = jnp.pad(current, ((3, 3), (0, 0), (0, 0)), mode='wrap')
        padded = jnp.pad(padded, ((0, 0), (3, 3), (0, 0)))

        def strip(start_tile, padded=padded, current=current, layer=layer):
            start = (start_tile * TILE).astype(jnp.int32)
            block = lax.dynamic_slice_in_dim(padded, start, TILE + 6, 0)
            convolved = depthwise(block, conv_weight[layer], TILE, NLAT)
            branch = mix_rows(convolved.reshape(-1, C), norm_gain[layer], norm_bias[layer], inner_weight[layer], inner_bias[layer], outer_weight[layer], outer_bias[layer]).reshape(TILE, NLAT, C)
            base = lax.dynamic_slice_in_dim(current, start, TILE, 0)
            wet_strip = lax.dynamic_slice_in_dim(cell_wet, start, TILE, 0)
            summed = (base.astype(jnp.float32) + branch.astype(jnp.float32)).astype(jnp.bfloat16)
            return jnp.where(wet_strip, summed, jnp.zeros((), jnp.bfloat16))
        current = lax.map(strip, jnp.arange(GLON, dtype=jnp.int32)).reshape(NLON, NLAT, C)
    return current
```

```python
import functools

import jax
import jax.numpy as jnp
from jax import lax
from jax.experimental import pallas as pl
from jax.experimental.pallas import tpu as pltpu
from jax.sharding import PartitionSpec as P

PHASE_I = 8
PHASE_J = 2
SEG = 16
STRIPS = 16
LEFT = 8


def swap_segments(parts):
    parts = list(parts)
    lane = lax.broadcasted_iota(jnp.int32, parts[0].shape, 1)
    for dist in (4, 2, 1):
        low_side = (lane // (SEG * dist)) % 2 == 0
        for p in range(8):
            if p & dist:
                continue
            low, high = parts[p], parts[p + dist]
            parts[p] = jnp.where(low_side, low, pltpu.roll(high, SEG * dist, 1))
            parts[p + dist] = jnp.where(low_side, pltpu.roll(low, 128 - SEG * dist, 1), high)
    return parts


def layer_body(
    wet_ref,
    state_ref,
    top_ref,
    bottom_ref,
    west_ref,
    east_ref,
    conv_ref,
    gain_ref,
    bias_ref,
    inner_ref,
    inner_bias_ref,
    outer_ref,
    outer_bias_ref,
    out_ref,
    wide_ref,
    taps_ref,
    rows_ref,
    band_ref,
    phased_ref,
    grouped_ref,
    cells_ref,
    branch_ref,
    *,
    tile,
):
    height, width, channels = state_ref.shape
    groups = channels // SEG
    blocks = height // PHASE_I
    steps = width // STRIPS
    pairs = steps // PHASE_J
    bf16 = jnp.bfloat16
    f32 = jnp.float32

    wide_ref[0:3, LEFT : LEFT + width, :] = top_ref[...].astype(f32)
    wide_ref[height + 3 : height + 6, LEFT : LEFT + width, :] = bottom_ref[...].astype(f32)
    wide_ref[height + 6 :] = jnp.zeros((2,) + wide_ref.shape[1:], f32)
    wide_ref[0 : height + 6, LEFT - 3 : LEFT, :] = west_ref[...].astype(f32)
    wide_ref[0 : height + 6, LEFT + width : LEFT + width + 3, :] = east_ref[...].astype(f32)

    def widen(i, carry):
        for tj in range(width // tile):
            wet = wet_ref[i // tile, tj] > 0
            piece = state_ref[i, tj * tile : (tj + 1) * tile, :].astype(f32)
            wide_ref[i + 3, LEFT + tj * tile : LEFT + (tj + 1) * tile, :] = jnp.where(
                wet, piece, 0.0
            )
        return carry

    lax.fori_loop(0, height, widen, 0, unroll=4)

    taps_ref[...] = jnp.zeros(taps_ref.shape, f32)
    taps_ref[7:14, 8:15, :] = conv_ref[...].astype(f32)

    def tap_rows(q, carry):
        for half in range(2):
            parts = []
            for p in range(8):
                pi, pj = (half * 8 + p) // 2, (half * 8 + p) % 2
                parts.append(taps_ref[q - pi + 7, pl.ds(8 - pj, 8), :])
            for g, part in enumerate(swap_segments(parts)):
                rows_ref[g, q, :, half * 128 : half * 128 + 128] = part
        return carry

    lax.fori_loop(0, 2 * PHASE_I, tap_rows, 0)

    lane = lax.broadcasted_iota(jnp.int32, (SEG, 256), 1)
    own = lax.broadcasted_iota(jnp.int32, (SEG, 256), 0) == lane % SEG

    def band(gq, carry):
        g, q = gq // (2 * PHASE_I), gq % (2 * PHASE_I)
        kb, pi = q // PHASE_I, q % PHASE_I
        for r in range(8):
            ub, pj = r // 2, r % 2
            row = jnp.broadcast_to(rows_ref[g, q, r : r + 1, :], (SEG, 256))
            band_ref[g, kb * 4 + ub, pl.ds((pi * 2 + pj) * SEG, SEG), :] = jnp.where(
                own, row, 0.0
            ).astype(bf16)
        return carry

    lax.fori_loop(0, groups * 2 * PHASE_I, band, 0, unroll=2)

    def to_phases(blk, carry):
        for u in range(pairs + 3):
            for half in range(2):
                parts = []
                for p in range(8):
                    pi, pj = (half * 8 + p) // 2, (half * 8 + p) % 2
                    strip = wide_ref[
                        blk * PHASE_I + pi, pl.ds(LEFT - 3 + 2 * u + pj, STRIPS, stride=steps), :
                    ]
                    parts.append(strip.astype(bf16))
                for g, part in enumerate(swap_segments(parts)):
                    phased_ref[g, blk, u, :, half * 128 : half * 128 + 128] = part
        return carry

    lax.fori_loop(0, blocks + 1, to_phases, 0)

    def convolve(g, carry):
        slabs = []
        mats = []
        for kb in range(2):
            for ub in range(4):
                slab = phased_ref[g, kb : kb + blocks, ub : ub + pairs]
                slabs.append(slab.reshape(blocks * pairs * STRIPS, 256))
                mats.append(band_ref[g, kb * 4 + ub])
        total = jnp.dot(
            jnp.concatenate(slabs, axis=1),
            jnp.concatenate(mats, axis=0),
            preferred_element_type=f32,
        )
        grouped_ref[g] = total.astype(bf16).reshape(blocks, pairs, STRIPS, 256)
        return carry

    lax.fori_loop(0, groups, convolve, 0)

    ones = jnp.full((channels, channels), 1.0 / channels, bf16)

    def mix(blk, carry):
        for v in range(pairs):
            for half in range(2):
                parts = swap_segments(
                    [grouped_ref[g, blk, v, :, half * 128 : half * 128 + 128] for g in range(groups)]
                )
                for p in range(8):
                    pi, pj = (half * 8 + p) // 2, (half * 8 + p) % 2
                    cells_ref[pi, 2 * v + pj] = parts[p]
        for quarter in range(4):
            conv = cells_ref[2 * quarter : 2 * quarter + 2].reshape(2 * width, channels)
            mean = jnp.dot(conv, ones, preferred_element_type=f32)
            centered = conv.astype(f32) - mean
            var = jnp.dot((centered * centered).astype(bf16), ones, preferred_element_type=f32)
            normed = (
                centered * lax.rsqrt(var + 1e-06) * gain_ref[...] + bias_ref[...]
            ).astype(bf16)
            pre = jnp.dot(normed, inner_ref[...], preferred_element_type=f32) + inner_bias_ref[...]
            hidden = (pre * (0.5 + 0.5 * lax.erf(pre * 0.7071067811865476))).astype(bf16)
            branch = (
                jnp.dot(hidden, outer_ref[...], preferred_element_type=f32) + outer_bias_ref[...]
            )
            branch_ref[2 * quarter : 2 * quarter + 2] = branch.astype(bf16).astype(f32).reshape(
                2, width, channels
            )
        for pi in range(PHASE_I):
            i = blk * PHASE_I + pi
            for s in range(0, STRIPS, 2):
                wet = wet_ref[blk * PHASE_I // tile, s * steps // tile] > 0
                delta = jnp.concatenate(
                    [branch_ref[pi, pl.ds(s + k, steps, stride=STRIPS), :] for k in range(2)], axis=0
                )
                base = state_ref[i, s * steps : (s + 2) * steps, :].astype(f32)
                out_ref[i, s * steps : (s + 2) * steps, :] = jnp.where(
                    wet, base + delta, 0.0
                ).astype(bf16)
        return carry

    lax.fori_loop(0, blocks, mix, 0)


def layer_call(wet, state, top, bottom, west, east, weights, tile):
    height, width, channels = state.shape
    groups = channels // SEG
    blocks = height // PHASE_I
    steps = width // STRIPS
    pairs = steps // PHASE_J
    assert channels == 128 and steps == 8 and height % PHASE_I == 0
    vmem = pl.BlockSpec(memory_space=pltpu.VMEM)
    smem = pl.BlockSpec(memory_space=pltpu.SMEM)

    return pl.pallas_call(
        functools.partial(layer_body, tile=tile),
        out_shape=jax.ShapeDtypeStruct(state.shape, jnp.bfloat16),
        in_specs=[smem] + [vmem] * 12,
        out_specs=vmem,
        scratch_shapes=[
            pltpu.VMEM((height + 8, width + 16, channels), jnp.float32),
            pltpu.VMEM((24, 24, channels), jnp.float32),
            pltpu.VMEM((groups, 2 * PHASE_I, 8, 256), jnp.float32),
            pltpu.VMEM((groups, 8, 256, 256), jnp.bfloat16),
            pltpu.VMEM((groups, blocks + 1, pairs + 3, STRIPS, 256), jnp.bfloat16),
            pltpu.VMEM((groups, blocks, pairs, STRIPS, 256), jnp.bfloat16),
            pltpu.VMEM((PHASE_I, steps, STRIPS, channels), jnp.bfloat16),
            pltpu.VMEM((PHASE_I, width, channels), jnp.float32),
        ],
        compiler_params=pltpu.CompilerParams(vmem_limit_bytes=48 << 20),
        name="block",
    )(wet, state, top, bottom, west, east, *weights)


def shift_pair(head, tail, axis, closed):
    count = lax.axis_size(axis)
    ends = count if closed else count - 1
    before = lax.ppermute(tail, axis, [(i, (i + 1) % count) for i in range(ends)])
    after = lax.ppermute(head, axis, [((i + 1) % count, i) for i in range(ends)])
    return before, after


def per_device(
    ocean_field,
    wet_tiles,
    conv_weight,
    norm_gain,
    norm_bias,
    inner_weight,
    inner_bias,
    outer_weight,
    outer_bias,
):
    tile = ocean_field.shape[0] // wet_tiles.shape[0]
    state = ocean_field
    for layer in range(conv_weight.shape[0]):
        if layer == 0:
            cell_wet = (
                jnp.repeat(jnp.repeat(wet_tiles, tile, axis=0), tile, axis=1)[:, :, None] > 0
            )
            edges = jnp.where(cell_wet, state, jnp.zeros((), state.dtype))
        else:
            edges = state
        top, bottom = shift_pair(edges[:3], edges[-3:], "lon", True)
        west, east = shift_pair(
            jnp.concatenate([top[:, :3], edges[:, :3], bottom[:, :3]], axis=0),
            jnp.concatenate([top[:, -3:], edges[:, -3:], bottom[:, -3:]], axis=0),
            "lat",
            False,
        )
        weights = (
            conv_weight[layer],
            norm_gain[layer][None],
            norm_bias[layer][None],
            inner_weight[layer],
            inner_bias[layer][None],
            outer_weight[layer],
            outer_bias[layer][None],
        )
        state = layer_call(wet_tiles, state, top, bottom, west, east, weights, tile)
    return state


def solution(mesh):
    return jax.shard_map(
        per_device,
        mesh=mesh,
        in_specs=(P("lon", "lat", None), P("lon", "lat"), P(), P(), P(), P(), P(), P(), P()),
        out_specs=P("lon", "lat", None),
        check_vma=False,
    )
```

```python
import functools

import jax
import jax.numpy as jnp
from jax import lax
from jax.experimental import pallas as pl
from jax.experimental.pallas import tpu as pltpu
from jax.sharding import PartitionSpec as P

PHASE_I = 8
PHASE_J = 2
SEG = 16
STRIPS = 16
LEFT = 8
ROWS = 8


def swap_segments(parts, back=False):
    parts = list(parts)
    lane = lax.broadcasted_iota(jnp.int32, parts[0].shape, 1)
    for dist in (1, 2, 4) if back else (4, 2, 1):
        low_side = (lane // (SEG * dist)) % 2 == 0
        turn = 128 - SEG * dist if back else SEG * dist
        for p in range(8):
            if p & dist:
                continue
            low, high = parts[p], parts[p + dist]
            moved = pltpu.roll(jnp.where(low_side, high, low), turn, 1)
            parts[p] = jnp.where(low_side, low, moved)
            parts[p + dist] = jnp.where(low_side, moved, high)
    return parts


def lane_slot(g, p):
    p1, p2, p4 = p & 1, p >> 1 & 1, p >> 2 & 1
    high = p4 ^ ((g >> 1) & (1 - p2))
    return ((high * 2 + p2 + (g & (1 - p1))) & 3) * 2 + p1


def layer_body(
    wet_ref,
    state_ref,
    top_ref,
    bottom_ref,
    west_ref,
    east_ref,
    conv_ref,
    gain_ref,
    bias_ref,
    inner_ref,
    inner_bias_ref,
    outer_ref,
    outer_bias_ref,
    out_ref,
    wide_ref,
    taps_ref,
    rows_ref,
    band_ref,
    phased_ref,
    grouped_ref,
    cells_ref,
    branch_ref,
    average_ref,
    center_ref,
    *,
    tile,
):
    height, width, channels = state_ref.shape
    groups = channels // SEG
    blocks = height // PHASE_I
    steps = width // STRIPS
    pairs = steps // PHASE_J
    bf16 = jnp.bfloat16
    f32 = jnp.float32

    wide_ref[0:3, LEFT : LEFT + width, :] = top_ref[...].astype(f32)
    wide_ref[height + 3 : height + 6, LEFT : LEFT + width, :] = bottom_ref[...].astype(f32)
    wide_ref[height + 6 :] = jnp.zeros((2,) + wide_ref.shape[1:], f32)
    wide_ref[0 : height + 6, LEFT - 3 : LEFT, :] = west_ref[...].astype(f32)
    wide_ref[0 : height + 6, LEFT + width : LEFT + width + 3, :] = east_ref[...].astype(f32)

    def widen(i, carry):
        for tj in range(width // tile):
            wet = wet_ref[i // tile, tj] > 0
            piece = state_ref[i, tj * tile : (tj + 1) * tile, :].astype(f32)
            wide_ref[i + 3, LEFT + tj * tile : LEFT + (tj + 1) * tile, :] = jnp.where(
                wet, piece, 0.0
            )
        return carry

    lax.fori_loop(0, height, widen, 0, unroll=4)

    taps_ref[...] = jnp.zeros(taps_ref.shape, f32)
    taps_ref[7:14, 8:15, :] = conv_ref[...].astype(f32)

    def tap_rows(q, carry):
        for half in range(2):
            parts = []
            for p in range(8):
                pi, pj = (half * 8 + p) // 2, (half * 8 + p) % 2
                parts.append(taps_ref[q - pi + 7, pl.ds(8 - pj, 8), :])
            for g, part in enumerate(swap_segments(parts)):
                rows_ref[g, q, :, half * 128 : half * 128 + 128] = part
        return carry

    lax.fori_loop(0, 2 * PHASE_I, tap_rows, 0)

    lane = lax.broadcasted_iota(jnp.int32, (SEG, 256), 1)
    own = lax.broadcasted_iota(jnp.int32, (SEG, 256), 0) == lane % SEG

    def band(step, carry):
        g, kb = step >> 1, step & 1
        for p in range(16):
            slot = (p >> 3) * 8 + lane_slot(g, p & 7)
            for ub in range(4):
                r = 2 * ub + (p & 1)
                row = rows_ref[g, kb * PHASE_I + (p >> 1), r : r + 1, :]
                band_ref[g, kb * 4 + ub, pl.ds(pl.multiple_of(slot * SEG, SEG), SEG), :] = jnp.where(
                    own, jnp.broadcast_to(row, (SEG, 256)), 0.0
                ).astype(bf16)
        return carry

    lax.fori_loop(0, groups * 2, band, 0)

    def to_phases(blk, carry):
        for u in range(pairs + 3):
            for half in range(2):
                parts = []
                for p in range(8):
                    pi, pj = (half * 8 + p) // 2, (half * 8 + p) % 2
                    strip = wide_ref[
                        blk * PHASE_I + pi, pl.ds(LEFT - 3 + 2 * u + pj, STRIPS, stride=steps), :
                    ]
                    parts.append(strip.astype(bf16))
                for g, part in enumerate(swap_segments(parts)):
                    phased_ref[g, blk, u, :, half * 128 : half * 128 + 128] = part
        return carry

    lax.fori_loop(0, blocks + 1, to_phases, 0)

    def convolve(g, carry):
        slabs = []
        mats = []
        for kb in range(2):
            for ub in range(4):
                slab = phased_ref[g, kb : kb + blocks, ub : ub + pairs]
                slabs.append(slab.reshape(blocks * pairs * STRIPS, 256))
                mats.append(band_ref[g, kb * 4 + ub])
        total = jnp.dot(
            jnp.concatenate(slabs, axis=1),
            jnp.concatenate(mats, axis=0),
            preferred_element_type=f32,
        )
        grouped_ref[g] = total.astype(bf16).reshape(blocks, pairs, STRIPS, 256)
        return carry

    lax.fori_loop(0, groups, convolve, 0)

    row = lax.broadcasted_iota(jnp.int32, (256, 256), 0)
    col = lax.broadcasted_iota(jnp.int32, (256, 256), 1)
    share = jnp.where(row // channels == col // channels, 1.0 / channels, 0.0)
    average_ref[...] = share.astype(bf16)
    center_ref[...] = (jnp.where(row == col, 1.0, 0.0) - share).astype(bf16)

    def mix(blk, carry):
        for v in range(pairs):
            for half in range(2):
                parts = swap_segments(
                    [grouped_ref[g, blk, v, :, half * 128 : half * 128 + 128] for g in range(groups)],
                    back=True,
                )
                for p in range(8):
                    pi, pj = (half * 8 + p) // 2, (half * 8 + p) % 2
                    cells_ref[pi, v, :, pj * channels : (pj + 1) * channels] = parts[p]
        for part in range(PHASE_I // ROWS):
            first = part * ROWS
            count = ROWS * pairs * STRIPS
            conv = cells_ref[first : first + ROWS].reshape(count, 2 * channels)
            centered = jnp.dot(conv, center_ref[...], preferred_element_type=f32)
            var = jnp.dot(
                (centered * centered).astype(bf16), average_ref[...], preferred_element_type=f32
            )
            normed = (
                centered * lax.rsqrt(var + 1e-06) * gain_ref[...] + bias_ref[...]
            ).astype(bf16)
            for pj in range(PHASE_J):
                pre = (
                    jnp.dot(
                        normed[:, pj * channels : (pj + 1) * channels],
                        inner_ref[...],
                        preferred_element_type=f32,
                    )
                    + inner_bias_ref[...]
                )
                hidden = (pre * (0.5 + 0.5 * lax.erf(pre * 0.7071067811865476))).astype(bf16)
                branch = (
                    jnp.dot(hidden, outer_ref[...], preferred_element_type=f32)
                    + outer_bias_ref[...]
                )
                branch = branch.astype(bf16).astype(f32).reshape(ROWS, pairs, STRIPS, channels)
                for pi in range(ROWS):
                    for v in range(pairs):
                        start = (2 * v + pj) * STRIPS
                        branch_ref[first + pi, start : start + STRIPS, :] = branch[pi, v]
        for pi in range(PHASE_I):
            i = blk * PHASE_I + pi
            for s in range(0, STRIPS, 2):
                wet = wet_ref[blk * PHASE_I // tile, s * steps // tile] > 0
                delta = jnp.concatenate(
                    [branch_ref[pi, pl.ds(s + k, steps, stride=STRIPS), :] for k in range(2)], axis=0
                )
                base = state_ref[i, s * steps : (s + 2) * steps, :].astype(f32)
                out_ref[i, s * steps : (s + 2) * steps, :] = jnp.where(
                    wet, base + delta, 0.0
                ).astype(bf16)
        return carry

    lax.fori_loop(0, blocks, mix, 0)


def layer_call(wet, state, top, bottom, west, east, weights, tile):
    height, width, channels = state.shape
    groups = channels // SEG
    blocks = height // PHASE_I
    steps = width // STRIPS
    pairs = steps // PHASE_J
    assert channels == 128 and steps == 8 and height % PHASE_I == 0
    vmem = pl.BlockSpec(memory_space=pltpu.VMEM)
    smem = pl.BlockSpec(memory_space=pltpu.SMEM)

    return pl.pallas_call(
        functools.partial(layer_body, tile=tile),
        out_shape=jax.ShapeDtypeStruct(state.shape, jnp.bfloat16),
        in_specs=[smem] + [vmem] * 12,
        out_specs=vmem,
        scratch_shapes=[
            pltpu.VMEM((height + 8, width + 16, channels), jnp.float32),
            pltpu.VMEM((24, 24, channels), jnp.float32),
            pltpu.VMEM((groups, 2 * PHASE_I, 8, 256), jnp.float32),
            pltpu.VMEM((groups, 8, 256, 256), jnp.bfloat16),
            pltpu.VMEM((groups, blocks + 1, pairs + 3, STRIPS, 256), jnp.bfloat16),
            pltpu.VMEM((groups, blocks, pairs, STRIPS, 256), jnp.bfloat16),
            pltpu.VMEM((PHASE_I, pairs, STRIPS, 2 * channels), jnp.bfloat16),
            pltpu.VMEM((PHASE_I, width, channels), jnp.float32),
            pltpu.VMEM((256, 256), jnp.bfloat16),
            pltpu.VMEM((256, 256), jnp.bfloat16),
        ],
        compiler_params=pltpu.CompilerParams(vmem_limit_bytes=48 << 20),
        name="block",
    )(wet, state, top, bottom, west, east, *weights)


def shift_pair(head, tail, axis, closed):
    count = lax.axis_size(axis)
    ends = count if closed else count - 1
    before = lax.ppermute(tail, axis, [(i, (i + 1) % count) for i in range(ends)])
    after = lax.ppermute(head, axis, [((i + 1) % count, i) for i in range(ends)])
    return before, after


def per_device(
    ocean_field,
    wet_tiles,
    conv_weight,
    norm_gain,
    norm_bias,
    inner_weight,
    inner_bias,
    outer_weight,
    outer_bias,
):
    tile = ocean_field.shape[0] // wet_tiles.shape[0]
    state = ocean_field
    for layer in range(conv_weight.shape[0]):
        if layer == 0:
            cell_wet = (
                jnp.repeat(jnp.repeat(wet_tiles, tile, axis=0), tile, axis=1)[:, :, None] > 0
            )
            edges = jnp.where(cell_wet, state, jnp.zeros((), state.dtype))
        else:
            edges = state
        top, bottom = shift_pair(edges[:3], edges[-3:], "lon", True)
        west, east = shift_pair(
            jnp.concatenate([top[:, :3], edges[:, :3], bottom[:, :3]], axis=0),
            jnp.concatenate([top[:, -3:], edges[:, -3:], bottom[:, -3:]], axis=0),
            "lat",
            False,
        )
        weights = (
            conv_weight[layer],
            jnp.tile(norm_gain[layer][None], (1, 2)),
            jnp.tile(norm_bias[layer][None], (1, 2)),
            inner_weight[layer],
            inner_bias[layer][None],
            outer_weight[layer],
            outer_bias[layer][None],
        )
        state = layer_call(wet_tiles, state, top, bottom, west, east, weights, tile)
    return state


def solution(mesh):
    return jax.shard_map(
        per_device,
        mesh=mesh,
        in_specs=(P("lon", "lat", None), P("lon", "lat"), P(), P(), P(), P(), P(), P(), P()),
        out_specs=P("lon", "lat", None),
        check_vma=False,
    )
```

```python
import functools

import jax
import jax.numpy as jnp
from jax import lax
from jax.experimental import pallas as pl
from jax.experimental.pallas import tpu as pltpu
from jax.sharding import PartitionSpec as P

PHASE_I = 8
PHASE_J = 2
PHASES = PHASE_I * PHASE_J
SEG = 16
STRIPS = 16
LEFT = 8
REACH = 3
RIM = 2 * REACH
LANES = 128
WIDE = 256
CHUNKS = 8


def swap_segments(parts, back=False):
    parts = list(parts)
    lane = lax.broadcasted_iota(jnp.int32, parts[0].shape, 1)
    for dist in (1, 2, 4) if back else (4, 2, 1):
        low_side = (lane // (SEG * dist)) % 2 == 0
        turn = LANES - SEG * dist if back else SEG * dist
        for p in range(8):
            if p & dist:
                continue
            low, high = parts[p], parts[p + dist]
            moved = pltpu.roll(jnp.where(low_side, high, low), turn, 1)
            parts[p] = jnp.where(low_side, low, moved)
            parts[p + dist] = jnp.where(low_side, moved, high)
    return parts


def lane_slot(g, p):
    p1, p2, p4 = p & 1, p >> 1 & 1, p >> 2 & 1
    high = p4 ^ ((g >> 1) & (1 - p2))
    return ((high * 2 + p2 + (g & (1 - p1))) & 3) * 2 + p1


def band_body(conv_ref, band_ref, taps_ref, rows_ref):
    f32 = jnp.float32
    g = pl.program_id(0)

    @pl.when(g == 0)
    def _():
        taps_ref[...] = jnp.zeros(taps_ref.shape, f32)
        taps_ref[7:14, 8:15, :] = conv_ref[...].astype(f32)

        def tap_rows(q, carry):
            for half in range(2):
                parts = []
                for p in range(8):
                    pi, pj = (half * 8 + p) // 2, (half * 8 + p) % 2
                    parts.append(taps_ref[q - pi + 7, pl.ds(8 - pj, 8), :])
                for group, part in enumerate(swap_segments(parts)):
                    rows_ref[group, q, :, half * LANES : (half + 1) * LANES] = part
            return carry

        lax.fori_loop(0, 2 * PHASE_I, tap_rows, 0, unroll=4)

    lane = lax.broadcasted_iota(jnp.int32, (SEG, WIDE), 1)
    own = lax.broadcasted_iota(jnp.int32, (SEG, WIDE), 0) == lane % SEG
    for kb in range(2):
        for p in range(PHASES):
            slot = (p >> 3) * 8 + lane_slot(g, p & 7)
            for ub in range(4):
                r = 2 * ub + (p & 1)
                row = rows_ref[g, kb * PHASE_I + (p >> 1), r : r + 1, :]
                band_ref[0, kb * 4 + ub, pl.ds(pl.multiple_of(slot * SEG, SEG), SEG), :] = jnp.where(
                    own, jnp.broadcast_to(row, (SEG, WIDE)), 0.0
                ).astype(jnp.bfloat16)


def band_call(kernel):
    groups = kernel.shape[2] // SEG
    return pl.pallas_call(
        band_body,
        grid=(groups,),
        out_shape=jax.ShapeDtypeStruct((groups, CHUNKS, WIDE, WIDE), jnp.bfloat16),
        in_specs=[pl.BlockSpec(kernel.shape, lambda g: (0, 0, 0))],
        out_specs=pl.BlockSpec((1, CHUNKS, WIDE, WIDE), lambda g: (g, 0, 0, 0)),
        scratch_shapes=[
            pltpu.VMEM((24, 24, LANES), jnp.float32),
            pltpu.VMEM((groups, 2 * PHASE_I, 8, WIDE), jnp.float32),
        ],
        compiler_params=pltpu.CompilerParams(vmem_limit_bytes=16 << 20),
        cost_estimate=pl.CostEstimate(
            flops=16 << 20, bytes_accessed=groups * CHUNKS * WIDE * WIDE * 2, transcendentals=0
        ),
        name="bands",
    )(kernel)


def blocks_body(
    wet_ref,
    state_ref,
    top_ref,
    bottom_ref,
    west_ref,
    east_ref,
    band_a_ref,
    band_b_ref,
    gain_ref,
    bias_ref,
    inner_ref,
    inner_bias_ref,
    outer_ref,
    outer_bias_ref,
    out_ref,
    first_ref,
    second_ref,
    mask_ref,
    wets_ref,
    bands_ref,
    phased_ref,
    grouped_ref,
    cells_ref,
    branch_ref,
    average_ref,
    center_ref,
    sems,
    *,
    tile,
):
    height, width, channels = state_ref.shape
    groups = channels // SEG
    bf16 = jnp.bfloat16
    f32 = jnp.float32
    steps_a = cells_ref.shape[1] * PHASE_J
    steps_b = width // STRIPS
    blocks_a = grouped_ref.shape[1]
    blocks_b = height // PHASE_I
    tiles_i = height // tile
    tiles_j = width // tile

    copies = [
        pltpu.make_async_copy(src, bands_ref.at[layer], sems.at[layer])
        for layer, src in enumerate((band_a_ref, band_b_ref))
    ]
    for copy in copies:
        copy.start()

    rows = height + 2 * RIM
    first_ref[:, LEFT + width + RIM - 6 :, :] = jnp.zeros(
        (first_ref.shape[0], first_ref.shape[1] - LEFT - width - RIM + 6, channels), f32
    )
    first_ref[rows:] = jnp.zeros((first_ref.shape[0] - rows,) + first_ref.shape[1:], f32)
    first_ref[0:RIM, LEFT : LEFT + width, :] = top_ref[0:RIM].astype(f32)
    first_ref[height + RIM : rows, LEFT : LEFT + width, :] = bottom_ref[0:RIM].astype(f32)
    first_ref[0:rows, LEFT - RIM : LEFT, :] = west_ref[:, 0:RIM, :].astype(f32)
    first_ref[0:rows, LEFT + width : LEFT + width + RIM, :] = east_ref[:, 0:RIM, :].astype(f32)

    def widen(i, carry):
        for tj in range(tiles_j):
            wet = wet_ref[i // tile, tj] > 0
            piece = state_ref[i, tj * tile : (tj + 1) * tile, :].astype(f32)
            first_ref[i + RIM, LEFT + tj * tile : LEFT + (tj + 1) * tile, :] = jnp.where(
                wet, piece, 0.0
            )
        return carry

    lax.fori_loop(0, height, widen, 0, unroll=4)

    mask_ref[...] = jnp.zeros(mask_ref.shape, f32)
    for region in range(tiles_i + 2):
        if region == 0:
            mask_ref[region, LEFT : LEFT + width, :] = top_ref[RIM].astype(f32)
            edge = 0
        elif region == tiles_i + 1:
            mask_ref[region, LEFT : LEFT + width, :] = bottom_ref[RIM].astype(f32)
            edge = rows - 1
        else:
            for tj in range(tiles_j):
                flag = jnp.where(wet_ref[region - 1, tj] > 0, 1.0, 0.0)
                mask_ref[region, LEFT + tj * tile : LEFT + (tj + 1) * tile, :] = jnp.full(
                    (tile, channels), flag, f32
                )
            edge = RIM + (region - 1) * tile
        mask_ref[region, LEFT - REACH : LEFT, :] = jnp.broadcast_to(
            west_ref[edge, RIM : RIM + 1, :].astype(f32), (REACH, channels)
        )
        mask_ref[region, LEFT + width : LEFT + width + REACH, :] = jnp.broadcast_to(
            east_ref[edge, RIM : RIM + 1, :].astype(f32), (REACH, channels)
        )
        for t in range(steps_a):
            wets_ref[region, t] = mask_ref[
                region, pl.ds(LEFT - REACH + t, STRIPS, stride=steps_a), :
            ]

    row = lax.broadcasted_iota(jnp.int32, (WIDE, WIDE), 0)
    col = lax.broadcasted_iota(jnp.int32, (WIDE, WIDE), 1)
    share = jnp.where(row // channels == col // channels, 1.0 / channels, 0.0)
    average_ref[...] = share.astype(bf16)
    center_ref[...] = (jnp.where(row == col, 1.0, 0.0) - share).astype(bf16)

    def layer(index, source_ref, start, blocks, steps):
        pairs = steps // PHASE_J

        def to_phases(blk, carry):
            for u in range(pairs + 3):
                for half in range(2):
                    parts = []
                    for p in range(8):
                        pi, pj = (half * 8 + p) // 2, (half * 8 + p) % 2
                        strip = source_ref[
                            blk * PHASE_I + pi, pl.ds(start + 2 * u + pj, STRIPS, stride=steps), :
                        ]
                        parts.append(strip.astype(bf16))
                    for g, part in enumerate(swap_segments(parts)):
                        phased_ref[g, blk, u, :, half * LANES : (half + 1) * LANES] = part
            return carry

        lax.fori_loop(0, blocks + 1, to_phases, 0)
        copies[index].wait()

        def convolve(g, carry):
            slabs = []
            mats = []
            for kb in range(2):
                for ub in range(4):
                    slab = phased_ref[g, kb : kb + blocks, ub : ub + pairs]
                    slabs.append(slab.reshape(blocks * pairs * STRIPS, WIDE))
                    mats.append(bands_ref[index, g, kb * 4 + ub])
            total = jnp.dot(
                jnp.concatenate(slabs, axis=1),
                jnp.concatenate(mats, axis=0),
                preferred_element_type=f32,
            )
            grouped_ref[g, 0:blocks, 0:pairs] = total.astype(bf16).reshape(
                blocks, pairs, STRIPS, WIDE
            )
            return carry

        lax.fori_loop(0, groups, convolve, 0)

        def mix(blk, carry):
            for v in range(pairs):
                for half in range(2):
                    parts = swap_segments(
                        [
                            grouped_ref[g, blk, v, :, half * LANES : (half + 1) * LANES]
                            for g in range(groups)
                        ],
                        back=True,
                    )
                    for p in range(8):
                        pi, pj = (half * 8 + p) // 2, (half * 8 + p) % 2
                        cells_ref[pi, v, :, pj * channels : (pj + 1) * channels] = parts[p]
            count = PHASE_I * pairs * STRIPS
            conv = cells_ref[:, 0:pairs].reshape(count, 2 * channels)
            centered = jnp.dot(conv, center_ref[...], preferred_element_type=f32)
            var = jnp.dot(
                (centered * centered).astype(bf16), average_ref[...], preferred_element_type=f32
            )
            normed = (
                centered * lax.rsqrt(var + 1e-06) * gain_ref[index : index + 1]
                + bias_ref[index : index + 1]
            ).astype(bf16)
            for pj in range(PHASE_J):
                pre = (
                    jnp.dot(
                        normed[:, pj * channels : (pj + 1) * channels],
                        inner_ref[index],
                        preferred_element_type=f32,
                    )
                    + inner_bias_ref[index : index + 1]
                )
                hidden = (pre * (0.5 + 0.5 * lax.erf(pre * 0.7071067811865476))).astype(bf16)
                branch = (
                    jnp.dot(hidden, outer_ref[index], preferred_element_type=f32)
                    + outer_bias_ref[index : index + 1]
                )
                branch = branch.astype(bf16).astype(f32).reshape(
                    PHASE_I, pairs, STRIPS, channels
                )
                for pi in range(PHASE_I):
                    for v in range(pairs):
                        t = 2 * v + pj
                        if index == 0:
                            r = blk * PHASE_I + pi
                            region = jnp.int32(0)
                            for bound in range(REACH, REACH + height + 1, tile):
                                region += (r >= bound).astype(jnp.int32)
                            base = first_ref[
                                r + REACH, pl.ds(LEFT - REACH + t, STRIPS, stride=steps), :
                            ]
                            updated = (base + branch[pi, v]).astype(bf16).astype(f32)
                            second_ref[r, pl.ds(LEFT - REACH + t, STRIPS, stride=steps), :] = (
                                jnp.where(wets_ref[region, t] > 0.0, updated, 0.0)
                            )
                        else:
                            branch_ref[pi, t * STRIPS : (t + 1) * STRIPS, :] = branch[pi, v]
            if index == 1:
                for pi in range(PHASE_I):
                    i = blk * PHASE_I + pi
                    for s in range(0, STRIPS, 2):
                        wet = wet_ref[i // tile, s * steps // tile] > 0
                        delta = jnp.concatenate(
                            [
                                branch_ref[pi, pl.ds(s + k, steps, stride=STRIPS), :]
                                for k in range(2)
                            ],
                            axis=0,
                        )
                        base = second_ref[
                            i + REACH, LEFT + s * steps : LEFT + (s + 2) * steps, :
                        ]
                        out_ref[i, s * steps : (s + 2) * steps, :] = jnp.where(
                            wet, base + delta, 0.0
                        ).astype(bf16)
            return carry

        lax.fori_loop(0, blocks, mix, 0)

    layer(0, first_ref, LEFT - RIM, blocks_a, steps_a)
    layer(1, second_ref, LEFT - REACH, blocks_b, steps_b)


def blocks_call(wet, state, top, bottom, west, east, bands, weights, tile):
    height, width, channels = state.shape
    groups = channels // SEG
    steps_b = width // STRIPS
    blocks_a = pl.cdiv(height + 2 * REACH, PHASE_I)
    steps_a = PHASE_J * pl.cdiv(width + 2 * REACH, STRIPS * PHASE_J)
    pairs_a = steps_a // PHASE_J
    span = LEFT + STRIPS * steps_a
    regions = height // tile + 2
    assert channels == LANES and steps_b == 8 and height % PHASE_I == 0
    vmem = pl.BlockSpec(memory_space=pltpu.VMEM)
    smem = pl.BlockSpec(memory_space=pltpu.SMEM)
    hbm = pl.BlockSpec(memory_space=pl.ANY)
    return pl.pallas_call(
        functools.partial(blocks_body, tile=tile),
        out_shape=jax.ShapeDtypeStruct(state.shape, jnp.bfloat16),
        in_specs=[smem] + [vmem] * 5 + [hbm] * 2 + [vmem] * 6,
        out_specs=vmem,
        scratch_shapes=[
            pltpu.VMEM((PHASE_I * (blocks_a + 1), span, channels), jnp.float32),
            pltpu.VMEM((PHASE_I * blocks_a, span, channels), jnp.float32),
            pltpu.VMEM((regions, span, channels), jnp.float32),
            pltpu.VMEM((regions, steps_a, STRIPS, channels), jnp.float32),
            pltpu.VMEM((2, groups, CHUNKS, WIDE, WIDE), jnp.bfloat16),
            pltpu.VMEM((groups, blocks_a + 1, pairs_a + 3, STRIPS, WIDE), jnp.bfloat16),
            pltpu.VMEM((groups, blocks_a, pairs_a, STRIPS, WIDE), jnp.bfloat16),
            pltpu.VMEM((PHASE_I, pairs_a, STRIPS, 2 * channels), jnp.bfloat16),
            pltpu.VMEM((PHASE_I, width, channels), jnp.float32),
            pltpu.VMEM((WIDE, WIDE), jnp.bfloat16),
            pltpu.VMEM((WIDE, WIDE), jnp.bfloat16),
            pltpu.SemaphoreType.DMA((2,)),
        ],
        compiler_params=pltpu.CompilerParams(vmem_limit_bytes=60 << 20),
        name="blocks",
    )(wet, state, top, bottom, west, east, *bands, *weights)


def shift_pair(head, tail, axis, closed):
    count = lax.axis_size(axis)
    ends = count if closed else count - 1
    before = lax.ppermute(tail, axis, [(i, (i + 1) % count) for i in range(ends)])
    after = lax.ppermute(head, axis, [((i + 1) % count, i) for i in range(ends)])
    return before, after


def per_device(
    ocean_field,
    wet_tiles,
    conv_weight,
    norm_gain,
    norm_bias,
    inner_weight,
    inner_bias,
    outer_weight,
    outer_bias,
):
    height, _, channels = ocean_field.shape
    tile = height // wet_tiles.shape[0]
    dtype = ocean_field.dtype

    def rim_rows(edge, flags):
        wet = jnp.repeat(flags, tile)[None, :, None]
        kept = jnp.where(wet > 0, edge, jnp.zeros((), dtype))
        return jnp.concatenate(
            [kept, jnp.broadcast_to(wet, (1,) + edge.shape[1:]).astype(dtype)], axis=0
        )

    top, bottom = shift_pair(
        rim_rows(ocean_field[:RIM], wet_tiles[0]),
        rim_rows(ocean_field[-RIM:], wet_tiles[-1]),
        "lon",
        True,
    )

    def rim_cols(edge, flags, above, below):
        wet = jnp.repeat(flags, tile)[:, None, None]
        kept = jnp.where(wet > 0, edge, jnp.zeros((), dtype))
        middle = jnp.concatenate(
            [kept, jnp.broadcast_to(wet, (height, 1, channels)).astype(dtype)], axis=1
        )
        ends = [
            jnp.concatenate(
                [rim[:RIM], jnp.broadcast_to(rim[RIM:, :1], (RIM, 1, channels))], axis=1
            )
            for rim in (above, below)
        ]
        return jnp.concatenate([ends[0], middle, ends[1]], axis=0)

    west, east = shift_pair(
        rim_cols(ocean_field[:, :RIM], wet_tiles[:, 0], top[:, :RIM], bottom[:, :RIM]),
        rim_cols(ocean_field[:, -RIM:], wet_tiles[:, -1], top[:, -RIM:], bottom[:, -RIM:]),
        "lat",
        False,
    )
    bands = [band_call(conv_weight[layer]) for layer in range(conv_weight.shape[0])]
    weights = (
        jnp.tile(norm_gain, (1, 2)),
        jnp.tile(norm_bias, (1, 2)),
        inner_weight,
        inner_bias,
        outer_weight,
        outer_bias,
    )
    return blocks_call(wet_tiles, ocean_field, top, bottom, west, east, bands, weights, tile)


def solution(mesh):
    return jax.shard_map(
        per_device,
        mesh=mesh,
        in_specs=(P("lon", "lat", None), P("lon", "lat"), P(), P(), P(), P(), P(), P(), P()),
        out_specs=P("lon", "lat", None),
        check_vma=False,
    )
```

```python
import functools

import jax
import jax.numpy as jnp
from jax import lax
from jax.experimental import pallas as pl
from jax.experimental.pallas import tpu as pltpu
from jax.sharding import PartitionSpec as P

PHASE_I = 8
PHASE_J = 2
PHASES = PHASE_I * PHASE_J
SEG = 16
STRIPS = 16
LEFT = 8
REACH = 3
RIM = 2 * REACH
LANES = 128
WIDE = 256
CHUNKS = 8


def swap_segments(parts, back=False):
    parts = list(parts)
    lane = lax.broadcasted_iota(jnp.int32, parts[0].shape, 1)
    for dist in (1, 2, 4) if back else (4, 2, 1):
        low_side = (lane // (SEG * dist)) % 2 == 0
        turn = LANES - SEG * dist if back else SEG * dist
        for p in range(8):
            if p & dist:
                continue
            low, high = parts[p], parts[p + dist]
            moved = pltpu.roll(jnp.where(low_side, high, low), turn, 1)
            parts[p] = jnp.where(low_side, low, moved)
            parts[p + dist] = jnp.where(low_side, moved, high)
    return parts


def lane_slot(g, p):
    p1, p2, p4 = p & 1, p >> 1 & 1, p >> 2 & 1
    high = p4 ^ ((g >> 1) & (1 - p2))
    return ((high * 2 + p2 + (g & (1 - p1))) & 3) * 2 + p1


def band_body(conv_ref, band_ref, taps_ref, rows_ref):
    f32 = jnp.float32
    g = pl.program_id(0)

    @pl.when(g == 0)
    def _():
        taps_ref[...] = jnp.zeros(taps_ref.shape, f32)
        taps_ref[7:14, 8:15, :] = conv_ref[...].astype(f32)

        def tap_rows(q, carry):
            for half in range(2):
                parts = []
                for p in range(8):
                    pi, pj = (half * 8 + p) // 2, (half * 8 + p) % 2
                    parts.append(taps_ref[q - pi + 7, pl.ds(8 - pj, 8), :])
                for group, part in enumerate(swap_segments(parts)):
                    rows_ref[group, q, half] = part
            return carry

        lax.fori_loop(0, 2 * PHASE_I, tap_rows, 0, unroll=4)

    lane = lax.broadcasted_iota(jnp.int32, (SEG, LANES), 1)
    own = lax.broadcasted_iota(jnp.int32, (SEG, LANES), 0) == lane % SEG
    for kb in range(2):
        for p in range(PHASES):
            slot = (p >> 3) * 8 + lane_slot(g, p & 7)
            at = pl.ds(pl.multiple_of(slot * SEG, SEG), SEG)
            for ub in range(4):
                r = 2 * ub + (p & 1)
                for half in range(2):
                    row = rows_ref[g, kb * PHASE_I + (p >> 1), half, r : r + 1, :]
                    band_ref[0, kb * 4 + ub, half, at, :] = jnp.where(
                        own, jnp.broadcast_to(row, (SEG, LANES)), 0.0
                    ).astype(jnp.bfloat16)


def band_call(kernels, layer):
    groups = kernels.shape[3] // SEG
    return pl.pallas_call(
        band_body,
        grid=(groups,),
        out_shape=jax.ShapeDtypeStruct((groups, CHUNKS, 2, WIDE, LANES), jnp.bfloat16),
        in_specs=[pl.BlockSpec((None,) + kernels.shape[1:], lambda g: (layer, 0, 0, 0))],
        out_specs=pl.BlockSpec((1, CHUNKS, 2, WIDE, LANES), lambda g: (g, 0, 0, 0, 0)),
        scratch_shapes=[
            pltpu.VMEM((24, 24, LANES), jnp.float32),
            pltpu.VMEM((groups, 2 * PHASE_I, 2, 8, LANES), jnp.float32),
        ],
        compiler_params=pltpu.CompilerParams(vmem_limit_bytes=16 << 20),
        cost_estimate=pl.CostEstimate(
            flops=16 << 20, bytes_accessed=groups * CHUNKS * WIDE * WIDE * 2, transcendentals=0
        ),
        name="bands",
    )(kernels)


def rim_rows_body(wet_ref, upper_ref, lower_ref, head_ref, tail_ref, *, tile):
    for rows_ref, out_ref, ti in ((upper_ref, head_ref, 0), (lower_ref, tail_ref, wet_ref.shape[0] - 1)):
        height, width, channels = rows_ref.shape
        first = 0 if ti == 0 and rows_ref is upper_ref else height - RIM
        for tj in range(width // tile):
            wet = wet_ref[ti, tj] > 0
            at = slice(tj * tile, (tj + 1) * tile)
            for r in range(RIM):
                out_ref[r, at, :] = jnp.where(
                    wet, rows_ref[first + r, at, :].astype(jnp.float32), 0.0
                ).astype(jnp.bfloat16)
            out_ref[RIM, at, :] = jnp.full(
                (tile, channels), jnp.where(wet, 1.0, 0.0), jnp.float32
            ).astype(jnp.bfloat16)


def rim_rows_call(wet, state, tile):
    height, width, channels = state.shape
    shape = jax.ShapeDtypeStruct((RIM + 1, width, channels), jnp.bfloat16)
    last = height // 8 - 1
    return pl.pallas_call(
        functools.partial(rim_rows_body, tile=tile),
        grid=(1,),
        out_shape=[shape, shape],
        in_specs=[
            pl.BlockSpec(memory_space=pltpu.SMEM),
            pl.BlockSpec((8, width, channels), lambda i: (0, 0, 0)),
            pl.BlockSpec((8, width, channels), lambda i: (last, 0, 0)),
        ],
        out_specs=[pl.BlockSpec(shape.shape, lambda i: (0, 0, 0))] * 2,
        compiler_params=pltpu.CompilerParams(vmem_limit_bytes=8 << 20),
        name="rim_rows",
    )(wet, state, state)


def rim_cols_body(wet_ref, left_ref, right_ref, top_ref, bottom_ref, head_ref, tail_ref, *, tile):
    f32 = jnp.float32
    bf16 = jnp.bfloat16
    height, chunk, channels = left_ref.shape
    width = top_ref.shape[1]
    tiles_i, tiles_j = wet_ref.shape
    for cols_ref, out_ref, tj, first, side in (
        (left_ref, head_ref, 0, 0, 0),
        (right_ref, tail_ref, tiles_j - 1, chunk - RIM, width - RIM),
    ):
        for ti in range(tiles_i):
            wet = wet_ref[ti, tj] > 0
            at = slice(RIM + ti * tile, RIM + (ti + 1) * tile)
            piece = cols_ref[ti * tile : (ti + 1) * tile].astype(f32)
            kept = jnp.where(wet, piece[:, first : first + RIM], 0.0)
            flag = jnp.full((tile, 1, channels), jnp.where(wet, 1.0, 0.0), f32)
            out_ref[at] = jnp.concatenate([kept, flag], axis=1).astype(bf16)
        for rim_ref, at in ((top_ref, 0), (bottom_ref, height + RIM)):
            kept = rim_ref[0:RIM, side : side + RIM, :].astype(f32)
            flag = rim_ref[RIM : RIM + 1, side : side + 1, :].astype(f32)
            out_ref[at : at + RIM] = jnp.concatenate(
                [kept, jnp.broadcast_to(flag, (RIM, 1, channels))], axis=1
            ).astype(bf16)


def rim_cols_call(wet, state, top, bottom, tile):
    height, width, channels = state.shape
    shape = jax.ShapeDtypeStruct((height + 2 * RIM, RIM + 1, channels), jnp.bfloat16)
    last = width // 8 - 1
    whole = pl.BlockSpec(top.shape, lambda i: (0, 0, 0))
    return pl.pallas_call(
        functools.partial(rim_cols_body, tile=tile),
        grid=(1,),
        out_shape=[shape, shape],
        in_specs=[
            pl.BlockSpec(memory_space=pltpu.SMEM),
            pl.BlockSpec((height, 8, channels), lambda i: (0, 0, 0)),
            pl.BlockSpec((height, 8, channels), lambda i: (0, last, 0)),
            whole,
            whole,
        ],
        out_specs=[pl.BlockSpec(shape.shape, lambda i: (0, 0, 0))] * 2,
        compiler_params=pltpu.CompilerParams(vmem_limit_bytes=8 << 20),
        name="rim_cols",
    )(wet, state, state, top, bottom)


def blocks_body(
    wet_ref,
    state_ref,
    top_ref,
    bottom_ref,
    west_ref,
    east_ref,
    band_a_ref,
    band_b_ref,
    gain_ref,
    bias_ref,
    inner_ref,
    inner_bias_ref,
    outer_ref,
    outer_bias_ref,
    out_ref,
    first_ref,
    second_ref,
    mask_ref,
    wets_ref,
    phased_ref,
    grouped_ref,
    cells_ref,
    branch_ref,
    average_ref,
    center_ref,
    inner_wide_ref,
    outer_half_ref,
    *,
    tile,
):
    height, width, channels = state_ref.shape
    groups = channels // SEG
    bf16 = jnp.bfloat16
    f32 = jnp.float32
    steps_a = cells_ref.shape[2] * PHASE_J
    steps_b = width // STRIPS
    blocks_a = grouped_ref.shape[2]
    blocks_b = height // PHASE_I
    tiles_i = height // tile
    tiles_j = width // tile

    rows = height + 2 * RIM
    first_ref[:, LEFT + width + RIM - 6 :, :] = jnp.zeros(
        (first_ref.shape[0], first_ref.shape[1] - LEFT - width - RIM + 6, channels), f32
    )
    first_ref[rows:] = jnp.zeros((first_ref.shape[0] - rows,) + first_ref.shape[1:], f32)
    first_ref[0:RIM, LEFT : LEFT + width, :] = top_ref[0:RIM].astype(f32)
    first_ref[height + RIM : rows, LEFT : LEFT + width, :] = bottom_ref[0:RIM].astype(f32)
    first_ref[0:rows, LEFT - RIM : LEFT, :] = west_ref[:, 0:RIM, :].astype(f32)
    first_ref[0:rows, LEFT + width : LEFT + width + RIM, :] = east_ref[:, 0:RIM, :].astype(f32)

    def widen(i, carry):
        for tj in range(tiles_j):
            wet = wet_ref[i // tile, tj] > 0
            piece = state_ref[i, tj * tile : (tj + 1) * tile, :].astype(f32)
            first_ref[i + RIM, LEFT + tj * tile : LEFT + (tj + 1) * tile, :] = jnp.where(
                wet, piece, 0.0
            )
        return carry

    lax.fori_loop(0, height, widen, 0, unroll=4)

    mask_ref[...] = jnp.zeros(mask_ref.shape, f32)
    for region in range(tiles_i + 2):
        if region == 0:
            mask_ref[region, LEFT : LEFT + width, :] = top_ref[RIM].astype(f32)
            edge = 0
        elif region == tiles_i + 1:
            mask_ref[region, LEFT : LEFT + width, :] = bottom_ref[RIM].astype(f32)
            edge = rows - 1
        else:
            for tj in range(tiles_j):
                flag = jnp.where(wet_ref[region - 1, tj] > 0, 1.0, 0.0)
                mask_ref[region, LEFT + tj * tile : LEFT + (tj + 1) * tile, :] = jnp.full(
                    (tile, channels), flag, f32
                )
            edge = RIM + (region - 1) * tile
        mask_ref[region, LEFT - REACH : LEFT, :] = jnp.broadcast_to(
            west_ref[edge, RIM : RIM + 1, :].astype(f32), (REACH, channels)
        )
        mask_ref[region, LEFT + width : LEFT + width + REACH, :] = jnp.broadcast_to(
            east_ref[edge, RIM : RIM + 1, :].astype(f32), (REACH, channels)
        )
        for t in range(steps_a):
            wets_ref[region, t] = mask_ref[
                region, pl.ds(LEFT - REACH + t, STRIPS, stride=steps_a), :
            ]

    row = lax.broadcasted_iota(jnp.int32, (WIDE, WIDE), 0)
    col = lax.broadcasted_iota(jnp.int32, (WIDE, WIDE), 1)
    share = jnp.where(row // channels == col // channels, 1.0 / channels, 0.0)
    average_ref[...] = share.astype(bf16)
    center_ref[...] = (jnp.where(row == col, 1.0, 0.0) - share).astype(bf16)

    for index in range(2):
        hidden_dim = inner_ref.shape[2]
        inner_wide_ref[index, 0:channels, :] = inner_ref[index]
        rest = inner_bias_ref[index : index + 1]
        parts = []
        for _ in range(3):
            parts.append(rest.astype(bf16).astype(f32))
            rest = rest - parts[-1]
        which = lax.broadcasted_iota(jnp.int32, (channels, hidden_dim), 0)
        tail = jnp.zeros((channels, hidden_dim), f32)
        for k, part in enumerate(parts):
            tail = jnp.where(which == k, part, tail)
        inner_wide_ref[index, channels : 2 * channels, :] = tail.astype(bf16)
        outer_half_ref[index] = (outer_ref[index].astype(f32) * 0.5).astype(bf16)

    def layer(index, source_ref, band_ref, start, blocks, steps):
        pairs = steps // PHASE_J
        gain = jnp.concatenate([gain_ref[index : index + 1]] * 2, axis=1)
        shift = jnp.concatenate([bias_ref[index : index + 1]] * 2, axis=1)
        bias_lanes = jnp.where(
            lax.broadcasted_iota(jnp.int32, (PHASE_I * pairs * STRIPS, channels), 1) < 3, 1.0, 0.0
        ).astype(bf16)

        def to_phases(blk, carry):
            for u in range(pairs + 3):
                for half in range(2):
                    parts = []
                    for p in range(8):
                        pi, pj = (half * 8 + p) // 2, (half * 8 + p) % 2
                        strip = source_ref[
                            blk * PHASE_I + pi, pl.ds(start + 2 * u + pj, STRIPS, stride=steps), :
                        ]
                        parts.append(strip.astype(bf16))
                    for g, part in enumerate(swap_segments(parts)):
                        phased_ref[g, half, blk, u] = part
            return carry

        lax.fori_loop(0, blocks + 1, to_phases, 0)

        def convolve(g, carry):
            slabs = []
            mats = []
            for kb in range(2):
                for ub in range(4):
                    for half in range(2):
                        slab = phased_ref[g, half, kb : kb + blocks, ub : ub + pairs]
                        slabs.append(slab.reshape(blocks * pairs * STRIPS, LANES))
                    band = band_ref.at[g, kb * 4 + ub]
                    mats.append(jnp.concatenate([band[0], band[1]], axis=1))
            total = jnp.dot(
                jnp.concatenate(slabs, axis=1),
                jnp.concatenate(mats, axis=0),
                preferred_element_type=f32,
            ).astype(bf16)
            for half in range(2):
                grouped_ref[g, half, 0:blocks, 0:pairs] = total[
                    :, half * LANES : (half + 1) * LANES
                ].reshape(blocks, pairs, STRIPS, LANES)
            return carry

        lax.fori_loop(0, groups, convolve, 0)

        def mix(blk, carry):
            for v in range(pairs):
                for half in range(2):
                    parts = swap_segments(
                        [grouped_ref[g, half, blk, v] for g in range(groups)], back=True
                    )
                    for p in range(8):
                        pi, pj = (half * 8 + p) // 2, (half * 8 + p) % 2
                        cells_ref[pj, pi, v] = parts[p]
            count = PHASE_I * pairs * STRIPS
            conv = jnp.concatenate(
                [cells_ref[pj, :, 0:pairs].reshape(count, channels) for pj in range(PHASE_J)],
                axis=1,
            )
            centered = jnp.dot(conv, center_ref[...], preferred_element_type=f32)
            var = jnp.dot(
                (centered * centered).astype(bf16), average_ref[...], preferred_element_type=f32
            )
            normed = (
                centered * lax.rsqrt(var + 1e-06) * gain
                + shift
            ).astype(bf16)
            for pj in range(PHASE_J):
                pre = jnp.dot(
                    jnp.concatenate(
                        [normed[:, pj * channels : (pj + 1) * channels], bias_lanes], axis=1
                    ),
                    inner_wide_ref[index],
                    preferred_element_type=f32,
                )
                hidden = (pre * (1.0 + lax.erf(pre * 0.7071067811865476))).astype(bf16)
                branch = (
                    jnp.dot(hidden, outer_half_ref[index], preferred_element_type=f32)
                    + outer_bias_ref[index : index + 1]
                ).reshape(PHASE_I, pairs, STRIPS, channels)
                for pi in range(PHASE_I):
                    for v in range(pairs):
                        t = 2 * v + pj
                        if index == 0:
                            r = blk * PHASE_I + pi
                            region = jnp.int32(0)
                            for bound in range(REACH, REACH + height + 1, tile):
                                region += (r >= bound).astype(jnp.int32)
                            base = first_ref[
                                r + REACH, pl.ds(LEFT - REACH + t, STRIPS, stride=steps), :
                            ]
                            second_ref[r, pl.ds(LEFT - REACH + t, STRIPS, stride=steps), :] = (
                                base + branch[pi, v]
                            ) * wets_ref[region, t]
                        else:
                            branch_ref[pi, t * STRIPS : (t + 1) * STRIPS, :] = branch[pi, v]
            if index == 1:
                for pi in range(PHASE_I):
                    i = blk * PHASE_I + pi
                    for s in range(0, STRIPS, 2):
                        wet = wet_ref[i // tile, s * steps // tile] > 0
                        delta = jnp.concatenate(
                            [
                                branch_ref[pi, pl.ds(s + k, steps, stride=STRIPS), :]
                                for k in range(2)
                            ],
                            axis=0,
                        )
                        base = second_ref[
                            i + REACH, LEFT + s * steps : LEFT + (s + 2) * steps, :
                        ]
                        out_ref[i, s * steps : (s + 2) * steps, :] = jnp.where(
                            wet, base + delta, 0.0
                        ).astype(bf16)
            return carry

        lax.fori_loop(0, blocks, mix, 0)

    layer(0, first_ref, band_a_ref, LEFT - RIM, blocks_a, steps_a)
    layer(1, second_ref, band_b_ref, LEFT - REACH, blocks_b, steps_b)


def blocks_call(wet, state, top, bottom, west, east, bands, weights, tile):
    height, width, channels = state.shape
    groups = channels // SEG
    steps_b = width // STRIPS
    blocks_a = pl.cdiv(height + 2 * REACH, PHASE_I)
    steps_a = PHASE_J * pl.cdiv(width + 2 * REACH, STRIPS * PHASE_J)
    pairs_a = steps_a // PHASE_J
    span = LEFT + STRIPS * steps_a
    regions = height // tile + 2
    assert channels == LANES and steps_b == 8 and height % PHASE_I == 0
    vmem = pl.BlockSpec(memory_space=pltpu.VMEM)
    smem = pl.BlockSpec(memory_space=pltpu.SMEM)
    return pl.pallas_call(
        functools.partial(blocks_body, tile=tile),
        out_shape=jax.ShapeDtypeStruct(state.shape, jnp.bfloat16),
        in_specs=[smem] + [vmem] * 13,
        out_specs=vmem,
        scratch_shapes=[
            pltpu.VMEM((PHASE_I * (blocks_a + 1), span, channels), jnp.float32),
            pltpu.VMEM((PHASE_I * blocks_a, span, channels), jnp.float32),
            pltpu.VMEM((regions, span, channels), jnp.float32),
            pltpu.VMEM((regions, steps_a, STRIPS, channels), jnp.float32),
            pltpu.VMEM((groups, 2, blocks_a + 1, pairs_a + 3, STRIPS, LANES), jnp.bfloat16),
            pltpu.VMEM((groups, 2, blocks_a, pairs_a, STRIPS, LANES), jnp.bfloat16),
            pltpu.VMEM((PHASE_J, PHASE_I, pairs_a, STRIPS, channels), jnp.bfloat16),
            pltpu.VMEM((PHASE_I, width, channels), jnp.float32),
            pltpu.VMEM((WIDE, WIDE), jnp.bfloat16),
            pltpu.VMEM((WIDE, WIDE), jnp.bfloat16),
            pltpu.VMEM((2, 2 * channels, weights[2].shape[2]), jnp.bfloat16),
            pltpu.VMEM((2, weights[2].shape[2], channels), jnp.bfloat16),
        ],
        compiler_params=pltpu.CompilerParams(vmem_limit_bytes=30 << 20),
        name="blocks",
    )(wet, state, top, bottom, west, east, *bands, *weights)


def shift_pair(head, tail, axis, closed):
    count = lax.axis_size(axis)
    ends = count if closed else count - 1
    before = lax.ppermute(tail, axis, [(i, (i + 1) % count) for i in range(ends)])
    after = lax.ppermute(head, axis, [((i + 1) % count, i) for i in range(ends)])
    return before, after


def per_device(
    ocean_field,
    wet_tiles,
    conv_weight,
    norm_gain,
    norm_bias,
    inner_weight,
    inner_bias,
    outer_weight,
    outer_bias,
):
    tile = ocean_field.shape[0] // wet_tiles.shape[0]
    rows = rim_rows_call(wet_tiles, ocean_field, tile)
    top, bottom = shift_pair(*rows, "lon", True)
    cols = rim_cols_call(wet_tiles, ocean_field, top, bottom, tile)
    west, east = shift_pair(*cols, "lat", False)
    bands = []
    for layer in range(conv_weight.shape[0]):
        bands.append(band_call(conv_weight, layer))
    weights = (norm_gain, norm_bias, inner_weight, inner_bias, outer_weight, outer_bias)
    return blocks_call(wet_tiles, ocean_field, top, bottom, west, east, bands, weights, tile)


def solution(mesh):
    return jax.shard_map(
        per_device,
        mesh=mesh,
        in_specs=(P("lon", "lat", None), P("lon", "lat"), P(), P(), P(), P(), P(), P(), P()),
        out_specs=P("lon", "lat", None),
        check_vma=False,
    )
```

```python
import functools

import jax
import jax.numpy as jnp
from jax import lax
from jax.experimental import pallas as pl
from jax.experimental.pallas import tpu as pltpu
from jax.sharding import PartitionSpec as P

PHASE_I = 8
PHASE_J = 2
PHASES = PHASE_I * PHASE_J
SEG = 16
STRIPS = 16
LEFT = 8
REACH = 3
RIM = 2 * REACH
LANES = 128
WIDE = 256
CHUNKS = 8


def swap_segments(parts, back=False):
    parts = list(parts)
    lane = lax.broadcasted_iota(jnp.int32, parts[0].shape, 1)
    for dist in (1, 2, 4) if back else (4, 2, 1):
        low_side = (lane // (SEG * dist)) % 2 == 0
        turn = LANES - SEG * dist if back else SEG * dist
        for p in range(8):
            if p & dist:
                continue
            low, high = parts[p], parts[p + dist]
            moved = pltpu.roll(jnp.where(low_side, high, low), turn, 1)
            parts[p] = jnp.where(low_side, low, moved)
            parts[p + dist] = jnp.where(low_side, moved, high)
    return parts


def lane_slot(g, p):
    p1, p2, p4 = p & 1, p >> 1 & 1, p >> 2 & 1
    high = p4 ^ ((g >> 1) & (1 - p2))
    return ((high * 2 + p2 + (g & (1 - p1))) & 3) * 2 + p1


def band_body(conv_ref, band_ref, taps_ref, rows_ref):
    f32 = jnp.float32
    g = pl.program_id(0)

    @pl.when(g == 0)
    def _():
        taps_ref[...] = jnp.zeros(taps_ref.shape, f32)
        taps_ref[7:14, 8:15, :] = conv_ref[...].astype(f32)

        def tap_rows(q, carry):
            for half in range(2):
                parts = []
                for p in range(8):
                    pi, pj = (half * 8 + p) // 2, (half * 8 + p) % 2
                    parts.append(taps_ref[q - pi + 7, pl.ds(8 - pj, 8), :])
                for group, part in enumerate(swap_segments(parts)):
                    rows_ref[group, q, half] = part
            return carry

        lax.fori_loop(0, 2 * PHASE_I, tap_rows, 0, unroll=4)

    lane = lax.broadcasted_iota(jnp.int32, (SEG, LANES), 1)
    own = lax.broadcasted_iota(jnp.int32, (SEG, LANES), 0) == lane % SEG
    for kb in range(2):
        for p in range(PHASES):
            slot = (p >> 3) * 8 + lane_slot(g, p & 7)
            at = pl.ds(pl.multiple_of(slot * SEG, SEG), SEG)
            for ub in range(4):
                r = 2 * ub + (p & 1)
                for half in range(2):
                    row = rows_ref[g, kb * PHASE_I + (p >> 1), half, r : r + 1, :]
                    band_ref[0, kb * 4 + ub, half, at, :] = jnp.where(
                        own, jnp.broadcast_to(row, (SEG, LANES)), 0.0
                    ).astype(jnp.bfloat16)


def band_call(kernels, layer):
    groups = kernels.shape[3] // SEG
    return pl.pallas_call(
        band_body,
        grid=(groups,),
        out_shape=jax.ShapeDtypeStruct((groups, CHUNKS, 2, WIDE, LANES), jnp.bfloat16),
        in_specs=[pl.BlockSpec((None,) + kernels.shape[1:], lambda g: (layer, 0, 0, 0))],
        out_specs=pl.BlockSpec((1, CHUNKS, 2, WIDE, LANES), lambda g: (g, 0, 0, 0, 0)),
        scratch_shapes=[
            pltpu.VMEM((24, 24, LANES), jnp.float32),
            pltpu.VMEM((groups, 2 * PHASE_I, 2, 8, LANES), jnp.float32),
        ],
        compiler_params=pltpu.CompilerParams(vmem_limit_bytes=16 << 20),
        cost_estimate=pl.CostEstimate(
            flops=16 << 20, bytes_accessed=groups * CHUNKS * WIDE * WIDE * 2, transcendentals=0
        ),
        name="bands",
    )(kernels)


def rim_rows_body(wet_ref, upper_ref, lower_ref, head_ref, tail_ref, *, tile):
    for rows_ref, out_ref, ti in ((upper_ref, head_ref, 0), (lower_ref, tail_ref, wet_ref.shape[0] - 1)):
        height, width, channels = rows_ref.shape
        first = 0 if ti == 0 and rows_ref is upper_ref else height - RIM
        for tj in range(width // tile):
            wet = wet_ref[ti, tj] > 0
            at = slice(tj * tile, (tj + 1) * tile)
            for r in range(RIM):
                out_ref[r, at, :] = jnp.where(
                    wet, rows_ref[first + r, at, :].astype(jnp.float32), 0.0
                ).astype(jnp.bfloat16)
            out_ref[RIM, at, :] = jnp.full(
                (tile, channels), jnp.where(wet, 1.0, 0.0), jnp.float32
            ).astype(jnp.bfloat16)


def rim_rows_call(wet, state, tile):
    height, width, channels = state.shape
    shape = jax.ShapeDtypeStruct((RIM + 1, width, channels), jnp.bfloat16)
    last = height // 8 - 1
    return pl.pallas_call(
        functools.partial(rim_rows_body, tile=tile),
        grid=(1,),
        out_shape=[shape, shape],
        in_specs=[
            pl.BlockSpec(memory_space=pltpu.SMEM),
            pl.BlockSpec((8, width, channels), lambda i: (0, 0, 0)),
            pl.BlockSpec((8, width, channels), lambda i: (last, 0, 0)),
        ],
        out_specs=[pl.BlockSpec(shape.shape, lambda i: (0, 0, 0))] * 2,
        compiler_params=pltpu.CompilerParams(vmem_limit_bytes=8 << 20),
        name="rim_rows",
    )(wet, state, state)


def rim_cols_body(wet_ref, left_ref, right_ref, top_ref, bottom_ref, head_ref, tail_ref, *, tile):
    f32 = jnp.float32
    bf16 = jnp.bfloat16
    height, chunk, channels = left_ref.shape
    width = top_ref.shape[1]
    tiles_i, tiles_j = wet_ref.shape
    for cols_ref, out_ref, tj, first, side in (
        (left_ref, head_ref, 0, 0, 0),
        (right_ref, tail_ref, tiles_j - 1, chunk - RIM, width - RIM),
    ):
        for ti in range(tiles_i):
            wet = wet_ref[ti, tj] > 0
            at = slice(RIM + ti * tile, RIM + (ti + 1) * tile)
            piece = cols_ref[ti * tile : (ti + 1) * tile].astype(f32)
            kept = jnp.where(wet, piece[:, first : first + RIM], 0.0)
            flag = jnp.full((tile, 1, channels), jnp.where(wet, 1.0, 0.0), f32)
            out_ref[at] = jnp.concatenate([kept, flag], axis=1).astype(bf16)
        for rim_ref, at in ((top_ref, 0), (bottom_ref, height + RIM)):
            kept = rim_ref[0:RIM, side : side + RIM, :].astype(f32)
            flag = rim_ref[RIM : RIM + 1, side : side + 1, :].astype(f32)
            out_ref[at : at + RIM] = jnp.concatenate(
                [kept, jnp.broadcast_to(flag, (RIM, 1, channels))], axis=1
            ).astype(bf16)


def rim_cols_call(wet, state, top, bottom, tile):
    height, width, channels = state.shape
    shape = jax.ShapeDtypeStruct((height + 2 * RIM, RIM + 1, channels), jnp.bfloat16)
    last = width // 8 - 1
    whole = pl.BlockSpec(top.shape, lambda i: (0, 0, 0))
    return pl.pallas_call(
        functools.partial(rim_cols_body, tile=tile),
        grid=(1,),
        out_shape=[shape, shape],
        in_specs=[
            pl.BlockSpec(memory_space=pltpu.SMEM),
            pl.BlockSpec((height, 8, channels), lambda i: (0, 0, 0)),
            pl.BlockSpec((height, 8, channels), lambda i: (0, last, 0)),
            whole,
            whole,
        ],
        out_specs=[pl.BlockSpec(shape.shape, lambda i: (0, 0, 0))] * 2,
        compiler_params=pltpu.CompilerParams(vmem_limit_bytes=8 << 20),
        name="rim_cols",
    )(wet, state, state, top, bottom)


def blocks_body(
    wet_ref,
    state_ref,
    top_ref,
    bottom_ref,
    west_ref,
    east_ref,
    band_a_ref,
    band_b_ref,
    gain_ref,
    bias_ref,
    inner_ref,
    inner_bias_ref,
    outer_ref,
    outer_bias_ref,
    out_ref,
    first_ref,
    second_ref,
    mask_ref,
    wets_ref,
    branch_ref,
    average_ref,
    center_ref,
    inner_wide_ref,
    outer_half_ref,
    *,
    tile,
    phased_ref,
    grouped_ref,
    cells_ref,
    normed_ref,
):
    height, width, channels = state_ref.shape
    groups = channels // SEG
    bf16 = jnp.bfloat16
    f32 = jnp.float32
    steps_a = cells_ref.shape[2] * PHASE_J
    steps_b = width // STRIPS
    blocks_a = grouped_ref.shape[2]
    blocks_b = height // PHASE_I
    tiles_i = height // tile
    tiles_j = width // tile

    rows = height + 2 * RIM
    first_ref[:, LEFT + width + RIM - 6 :, :] = jnp.zeros(
        (first_ref.shape[0], first_ref.shape[1] - LEFT - width - RIM + 6, channels), f32
    )
    first_ref[rows:] = jnp.zeros((first_ref.shape[0] - rows,) + first_ref.shape[1:], f32)
    first_ref[0:RIM, LEFT : LEFT + width, :] = top_ref[0:RIM].astype(f32)
    first_ref[height + RIM : rows, LEFT : LEFT + width, :] = bottom_ref[0:RIM].astype(f32)
    first_ref[0:rows, LEFT - RIM : LEFT, :] = west_ref[:, 0:RIM, :].astype(f32)
    first_ref[0:rows, LEFT + width : LEFT + width + RIM, :] = east_ref[:, 0:RIM, :].astype(f32)

    def widen(i, carry):
        for tj in range(tiles_j):
            wet = wet_ref[i // tile, tj] > 0
            piece = state_ref[i, tj * tile : (tj + 1) * tile, :].astype(f32)
            first_ref[i + RIM, LEFT + tj * tile : LEFT + (tj + 1) * tile, :] = jnp.where(
                wet, piece, 0.0
            )
        return carry

    lax.fori_loop(0, height, widen, 0, unroll=4)

    mask_ref[...] = jnp.zeros(mask_ref.shape, f32)
    for region in range(tiles_i + 2):
        if region == 0:
            mask_ref[region, LEFT : LEFT + width, :] = top_ref[RIM].astype(f32)
            edge = 0
        elif region == tiles_i + 1:
            mask_ref[region, LEFT : LEFT + width, :] = bottom_ref[RIM].astype(f32)
            edge = rows - 1
        else:
            for tj in range(tiles_j):
                flag = jnp.where(wet_ref[region - 1, tj] > 0, 1.0, 0.0)
                mask_ref[region, LEFT + tj * tile : LEFT + (tj + 1) * tile, :] = jnp.full(
                    (tile, channels), flag, f32
                )
            edge = RIM + (region - 1) * tile
        mask_ref[region, LEFT - REACH : LEFT, :] = jnp.broadcast_to(
            west_ref[edge, RIM : RIM + 1, :].astype(f32), (REACH, channels)
        )
        mask_ref[region, LEFT + width : LEFT + width + REACH, :] = jnp.broadcast_to(
            east_ref[edge, RIM : RIM + 1, :].astype(f32), (REACH, channels)
        )
        for t in range(steps_a):
            wets_ref[region, t] = mask_ref[
                region, pl.ds(LEFT - REACH + t, STRIPS, stride=steps_a), :
            ]

    row = lax.broadcasted_iota(jnp.int32, (WIDE, WIDE), 0)
    col = lax.broadcasted_iota(jnp.int32, (WIDE, WIDE), 1)
    share = jnp.where(row // channels == col // channels, 1.0 / channels, 0.0)
    average_ref[...] = share.astype(bf16)
    center_ref[...] = (jnp.where(row == col, 1.0, 0.0) - share).astype(bf16)

    for index in range(2):
        hidden_dim = inner_ref.shape[2]
        inner_wide_ref[index, 0:channels, :] = inner_ref[index]
        rest = inner_bias_ref[index : index + 1]
        parts = []
        for _ in range(3):
            parts.append(rest.astype(bf16).astype(f32))
            rest = rest - parts[-1]
        which = lax.broadcasted_iota(jnp.int32, (channels, hidden_dim), 0)
        tail = jnp.zeros((channels, hidden_dim), f32)
        for k, part in enumerate(parts):
            tail = jnp.where(which == k, part, tail)
        inner_wide_ref[index, channels : 2 * channels, :] = tail.astype(bf16)
        outer_half_ref[index] = (outer_ref[index].astype(f32) * 0.5).astype(bf16)

    def layer(index, source_ref, band_ref, start, blocks, steps):
        pairs = steps // PHASE_J
        gain = jnp.concatenate([gain_ref[index : index + 1]] * 2, axis=1)
        shift = jnp.concatenate([bias_ref[index : index + 1]] * 2, axis=1)
        bias_lanes = jnp.where(
            lax.broadcasted_iota(jnp.int32, (PHASE_I * pairs * STRIPS, channels), 1) < 3, 1.0, 0.0
        ).astype(bf16)

        def to_phases(blk, carry):
            for u in range(pairs + 3):
                for half in range(2):
                    parts = []
                    for p in range(8):
                        pi, pj = (half * 8 + p) // 2, (half * 8 + p) % 2
                        strip = source_ref[
                            blk * PHASE_I + pi, pl.ds(start + 2 * u + pj, STRIPS, stride=steps), :
                        ]
                        parts.append(strip.astype(bf16))
                    for g, part in enumerate(swap_segments(parts)):
                        phased_ref[g, half, blk, u] = part
            return carry

        lax.fori_loop(0, blocks + 1, to_phases, 0)

        def convolve(g, carry):
            slabs = []
            mats = []
            for kb in range(2):
                for ub in range(4):
                    for half in range(2):
                        slab = phased_ref[g, half, kb : kb + blocks, ub : ub + pairs]
                        slabs.append(slab.reshape(blocks * pairs * STRIPS, LANES))
                    band = band_ref.at[g, kb * 4 + ub]
                    mats.append(jnp.concatenate([band[0], band[1]], axis=1))
            total = jnp.dot(
                jnp.concatenate(slabs, axis=1),
                jnp.concatenate(mats, axis=0),
                preferred_element_type=f32,
            ).astype(bf16)
            for half in range(2):
                grouped_ref[g, half, 0:blocks, 0:pairs] = total[
                    :, half * LANES : (half + 1) * LANES
                ].reshape(blocks, pairs, STRIPS, LANES)
            return carry

        lax.fori_loop(0, groups, convolve, 0, unroll=4)

        def to_cells(blk):
            for v in range(pairs):
                for half in range(2):
                    parts = swap_segments(
                        [grouped_ref[g, half, blk, v] for g in range(groups)], back=True
                    )
                    for p in range(8):
                        pi, pj = (half * 8 + p) // 2, (half * 8 + p) % 2
                        cells_ref[pj, pi, v] = parts[p]

        count = PHASE_I * pairs * STRIPS

        def normalize():
            conv = jnp.concatenate(
                [cells_ref[pj, :, 0:pairs].reshape(count, channels) for pj in range(PHASE_J)],
                axis=1,
            )
            centered = jnp.dot(conv, center_ref[...], preferred_element_type=f32)
            var = jnp.dot(
                (centered * centered).astype(bf16), average_ref[...], preferred_element_type=f32
            )
            normed = (centered * lax.rsqrt(var + 1e-06) * gain + shift).astype(bf16)
            for pj in range(PHASE_J):
                normed_ref[pj, 0:count] = normed[:, pj * channels : (pj + 1) * channels]

        def finish(blk):
            for pi in range(PHASE_I):
                i = blk * PHASE_I + pi
                for s in range(0, STRIPS, 2):
                    wet = wet_ref[i // tile, s * steps // tile] > 0
                    delta = jnp.concatenate(
                        [branch_ref[pi, pl.ds(s + k, steps, stride=STRIPS), :] for k in range(2)],
                        axis=0,
                    )
                    base = second_ref[i + REACH, LEFT + s * steps : LEFT + (s + 2) * steps, :]
                    out_ref[i, s * steps : (s + 2) * steps, :] = jnp.where(
                        wet, base + delta, 0.0
                    ).astype(bf16)

        def mix(blk, carry):
            if index == 1:
                finish(jnp.maximum(blk - 1, 0))
            for pj in range(PHASE_J):
                pre = jnp.dot(
                    jnp.concatenate([normed_ref[pj, 0:count], bias_lanes], axis=1),
                    inner_wide_ref[index],
                    preferred_element_type=f32,
                )
                hidden = (pre * (1.0 + lax.erf(pre * 0.7071067811865476))).astype(bf16)
                branch = (
                    jnp.dot(hidden, outer_half_ref[index], preferred_element_type=f32)
                    + outer_bias_ref[index : index + 1]
                ).reshape(PHASE_I, pairs, STRIPS, channels)
                for pi in range(PHASE_I):
                    for v in range(pairs):
                        t = 2 * v + pj
                        if index == 0:
                            r = blk * PHASE_I + pi
                            region = jnp.int32(0)
                            for bound in range(REACH, REACH + height + 1, tile):
                                region += (r >= bound).astype(jnp.int32)
                            base = first_ref[
                                r + REACH, pl.ds(LEFT - REACH + t, STRIPS, stride=steps), :
                            ]
                            second_ref[r, pl.ds(LEFT - REACH + t, STRIPS, stride=steps), :] = (
                                base + branch[pi, v]
                            ) * wets_ref[region, t]
                        else:
                            branch_ref[pi, t * STRIPS : (t + 1) * STRIPS, :] = branch[pi, v]
            normalize()
            to_cells(jnp.minimum(blk + 2, blocks - 1))
            return carry

        to_cells(0)
        normalize()
        to_cells(1)
        lax.fori_loop(0, blocks, mix, 0)
        if index == 1:
            finish(blocks - 1)

    layer(0, first_ref, band_a_ref, LEFT - RIM, blocks_a, steps_a)
    layer(1, second_ref, band_b_ref, LEFT - REACH, blocks_b, steps_b)


def blocks_call(wet, state, top, bottom, west, east, bands, weights, tile):
    height, width, channels = state.shape
    groups = channels // SEG
    steps_b = width // STRIPS
    blocks_a = pl.cdiv(height + 2 * REACH, PHASE_I)
    steps_a = PHASE_J * pl.cdiv(width + 2 * REACH, STRIPS * PHASE_J)
    pairs_a = steps_a // PHASE_J
    span = LEFT + STRIPS * steps_a
    regions = height // tile + 2
    assert channels == LANES and steps_b == 8 and height % PHASE_I == 0
    vmem = pl.BlockSpec(memory_space=pltpu.VMEM)
    smem = pl.BlockSpec(memory_space=pltpu.SMEM)
    packed = dict(
        phased_ref=pltpu.VMEM((groups, 2, blocks_a + 1, pairs_a + 3, STRIPS, LANES), jnp.bfloat16),
        grouped_ref=pltpu.VMEM((groups, 2, blocks_a, pairs_a, STRIPS, LANES), jnp.bfloat16),
        cells_ref=pltpu.VMEM((PHASE_J, PHASE_I, pairs_a, STRIPS, channels), jnp.bfloat16),
        normed_ref=pltpu.VMEM((PHASE_J, PHASE_I * pairs_a * STRIPS, channels), jnp.bfloat16),
    )

    def body(*refs):
        pl.run_scoped(functools.partial(blocks_body, *refs, tile=tile), **packed)

    return pl.pallas_call(
        body,
        out_shape=jax.ShapeDtypeStruct(state.shape, jnp.bfloat16),
        in_specs=[smem] + [vmem] * 13,
        out_specs=vmem,
        scratch_shapes=[
            pltpu.VMEM((PHASE_I * (blocks_a + 1), span, channels), jnp.float32),
            pltpu.VMEM((PHASE_I * blocks_a, span, channels), jnp.float32),
            pltpu.VMEM((regions, span, channels), jnp.float32),
            pltpu.VMEM((regions, steps_a, STRIPS, channels), jnp.float32),
            pltpu.VMEM((PHASE_I, width, channels), jnp.float32),
            pltpu.VMEM((WIDE, WIDE), jnp.bfloat16),
            pltpu.VMEM((WIDE, WIDE), jnp.bfloat16),
            pltpu.VMEM((2, 2 * channels, weights[2].shape[2]), jnp.bfloat16),
            pltpu.VMEM((2, weights[2].shape[2], channels), jnp.bfloat16),
        ],
        compiler_params=pltpu.CompilerParams(vmem_limit_bytes=30 << 20),
        name="blocks",
    )(wet, state, top, bottom, west, east, *bands, *weights)


def shift_pair(head, tail, axis, closed):
    count = lax.axis_size(axis)
    ends = count if closed else count - 1
    before = lax.ppermute(tail, axis, [(i, (i + 1) % count) for i in range(ends)])
    after = lax.ppermute(head, axis, [((i + 1) % count, i) for i in range(ends)])
    return before, after


def per_device(
    ocean_field,
    wet_tiles,
    conv_weight,
    norm_gain,
    norm_bias,
    inner_weight,
    inner_bias,
    outer_weight,
    outer_bias,
):
    tile = ocean_field.shape[0] // wet_tiles.shape[0]
    rows = rim_rows_call(wet_tiles, ocean_field, tile)
    top, bottom = shift_pair(*rows, "lon", True)
    cols = rim_cols_call(wet_tiles, ocean_field, top, bottom, tile)
    west, east = shift_pair(*cols, "lat", False)
    bands = []
    for layer in range(conv_weight.shape[0]):
        bands.append(band_call(conv_weight, layer))
    weights = (norm_gain, norm_bias, inner_weight, inner_bias, outer_weight, outer_bias)
    return blocks_call(wet_tiles, ocean_field, top, bottom, west, east, bands, weights, tile)


def solution(mesh):
    return jax.shard_map(
        per_device,
        mesh=mesh,
        in_specs=(P("lon", "lat", None), P("lon", "lat"), P(), P(), P(), P(), P(), P(), P()),
        out_specs=P("lon", "lat", None),
        check_vma=False,
    )
```

```python
import functools

import jax
import jax.numpy as jnp
from jax import lax
from jax.experimental import pallas as pl
from jax.experimental.pallas import tpu as pltpu
from jax.sharding import PartitionSpec as P

PHASE_I = 8
PHASE_J = 2
PHASES = PHASE_I * PHASE_J
SEG = 16
STRIPS = 16
LEFT = 8
REACH = 3
RIM = 2 * REACH
LANES = 128
WIDE = 256
CHUNKS = 8
INNER_MIB = 20
OUTER_MIB = 26
WHOLE_VMEM = 67043328


def swap_segments(parts, back=False):
    parts = list(parts)
    lane = lax.broadcasted_iota(jnp.int32, parts[0].shape, 1)
    for dist in (1, 2, 4) if back else (4, 2, 1):
        low_side = (lane // (SEG * dist)) % 2 == 0
        turn = LANES - SEG * dist if back else SEG * dist
        for p in range(8):
            if p & dist:
                continue
            low, high = parts[p], parts[p + dist]
            moved = pltpu.roll(jnp.where(low_side, high, low), turn, 1)
            parts[p] = jnp.where(low_side, low, moved)
            parts[p + dist] = jnp.where(low_side, moved, high)
    return parts


def lane_slot(g, p):
    p1, p2, p4 = p & 1, p >> 1 & 1, p >> 2 & 1
    high = p4 ^ ((g >> 1) & (1 - p2))
    return ((high * 2 + p2 + (g & (1 - p1))) & 3) * 2 + p1


def band_body(conv_ref, band_ref, taps_ref, rows_ref):
    f32 = jnp.float32
    g = pl.program_id(0)

    @pl.when(g == 0)
    def _():
        taps_ref[...] = jnp.zeros(taps_ref.shape, f32)
        taps_ref[7:14, 8:15, :] = conv_ref[...].astype(f32)

        def tap_rows(q, carry):
            for half in range(2):
                parts = []
                for p in range(8):
                    pi, pj = (half * 8 + p) // 2, (half * 8 + p) % 2
                    parts.append(taps_ref[q - pi + 7, pl.ds(8 - pj, 8), :])
                for group, part in enumerate(swap_segments(parts)):
                    rows_ref[group, q, half] = part
            return carry

        lax.fori_loop(0, 2 * PHASE_I, tap_rows, 0, unroll=4)

    lane = lax.broadcasted_iota(jnp.int32, (SEG, LANES), 1)
    own = lax.broadcasted_iota(jnp.int32, (SEG, LANES), 0) == lane % SEG
    for kb in range(2):
        for p in range(PHASES):
            slot = (p >> 3) * 8 + lane_slot(g, p & 7)
            at = pl.ds(pl.multiple_of(slot * SEG, SEG), SEG)
            for ub in range(4):
                r = 2 * ub + (p & 1)
                for half in range(2):
                    row = rows_ref[g, kb * PHASE_I + (p >> 1), half, r : r + 1, :]
                    band_ref[0, kb * 4 + ub, half, at, :] = jnp.where(
                        own, jnp.broadcast_to(row, (SEG, LANES)), 0.0
                    ).astype(jnp.bfloat16)


def band_call(kernels, layer):
    groups = kernels.shape[3] // SEG
    return pl.pallas_call(
        band_body,
        grid=(groups,),
        out_shape=jax.ShapeDtypeStruct((groups, CHUNKS, 2, WIDE, LANES), jnp.bfloat16),
        in_specs=[pl.BlockSpec((None,) + kernels.shape[1:], lambda g: (layer, 0, 0, 0))],
        out_specs=pl.BlockSpec((1, CHUNKS, 2, WIDE, LANES), lambda g: (g, 0, 0, 0, 0)),
        scratch_shapes=[
            pltpu.VMEM((24, 24, LANES), jnp.float32),
            pltpu.VMEM((groups, 2 * PHASE_I, 2, 8, LANES), jnp.float32),
        ],
        compiler_params=pltpu.CompilerParams(vmem_limit_bytes=16 << 20),
        cost_estimate=pl.CostEstimate(
            flops=16 << 20, bytes_accessed=groups * CHUNKS * WIDE * WIDE * 2, transcendentals=0
        ),
        name="bands",
    )(kernels)


def rim_cols_body(wet_hbm, state_hbm, head_ref, tail_ref, wet_ref, left_ref, right_ref, sems, *, tile):
    f32 = jnp.float32
    _, chunk, channels = left_ref.shape
    width = state_hbm.shape[1]
    copies = [
        pltpu.make_async_copy(wet_hbm, wet_ref, sems.at[0]),
        pltpu.make_async_copy(state_hbm.at[:, 0:chunk, :], left_ref, sems.at[1]),
        pltpu.make_async_copy(state_hbm.at[:, width - chunk : width, :], right_ref, sems.at[2]),
    ]
    for copy in copies:
        copy.start()
    for copy in copies:
        copy.wait()
    tiles_i, tiles_j = wet_ref.shape
    for cols_ref, out_ref, tj, first in (
        (left_ref, head_ref, 0, 0),
        (right_ref, tail_ref, tiles_j - 1, chunk - RIM),
    ):
        for ti in range(tiles_i):
            wet = wet_ref[ti, tj] > 0
            at = slice(ti * tile, (ti + 1) * tile)
            piece = cols_ref[at].astype(f32)
            kept = jnp.where(wet, piece[:, first : first + RIM], 0.0)
            flag = jnp.full((tile, 1, channels), jnp.where(wet, 1.0, 0.0), f32)
            out_ref[at] = jnp.concatenate([kept, flag], axis=1).astype(jnp.bfloat16)


def rim_cols_call(wet, state, tile):
    height, _, channels = state.shape
    shape = jax.ShapeDtypeStruct((height, RIM + 1, channels), jnp.bfloat16)
    vmem = pl.BlockSpec(memory_space=pltpu.VMEM)
    hbm = pl.BlockSpec(memory_space=pltpu.HBM)
    return pl.pallas_call(
        functools.partial(rim_cols_body, tile=tile),
        out_shape=[shape, shape],
        in_specs=[hbm, hbm],
        out_specs=[vmem, vmem],
        scratch_shapes=[
            pltpu.SMEM(wet.shape, jnp.int32),
            pltpu.VMEM((height, 8, channels), state.dtype),
            pltpu.VMEM((height, 8, channels), state.dtype),
            pltpu.SemaphoreType.DMA((3,)),
        ],
        compiler_params=pltpu.CompilerParams(vmem_limit_bytes=WHOLE_VMEM),
        name="rim_cols",
    )(wet, state)


def rim_rows_body(wet_ref, state_ref, west_ref, east_ref, head_ref, tail_ref, *, tile):
    f32 = jnp.float32
    bf16 = jnp.bfloat16
    height, width, channels = state_ref.shape
    for out_ref, ti, first in ((head_ref, 0, 0), (tail_ref, wet_ref.shape[0] - 1, height - RIM)):
        out_ref[:, 0:LEFT, :] = jnp.zeros((RIM + 1, LEFT, channels), bf16)
        out_ref[:, LEFT + width :, :] = jnp.zeros((RIM + 1, LEFT, channels), bf16)
        for side_ref, at in ((west_ref, LEFT - RIM), (east_ref, LEFT + width)):
            side = side_ref[first : first + RIM].astype(f32)
            out_ref[0:RIM, at : at + RIM, :] = side[:, 0:RIM].astype(bf16)
            out_ref[RIM, at : at + RIM, :] = jnp.broadcast_to(
                side[0, RIM : RIM + 1], (RIM, channels)
            ).astype(bf16)
        for tj in range(width // tile):
            wet = wet_ref[ti, tj] > 0
            at = slice(LEFT + tj * tile, LEFT + (tj + 1) * tile)
            for r in range(RIM):
                piece = state_ref[first + r, tj * tile : (tj + 1) * tile, :].astype(f32)
                out_ref[r, at, :] = jnp.where(wet, piece, 0.0).astype(bf16)
            out_ref[RIM, at, :] = jnp.full(
                (tile, channels), jnp.where(wet, 1.0, 0.0), f32
            ).astype(bf16)


def rim_rows_call(wet, state, west, east, tile):
    _, width, channels = state.shape
    shape = jax.ShapeDtypeStruct((RIM + 1, width + 2 * LEFT, channels), jnp.bfloat16)
    vmem = pl.BlockSpec(memory_space=pltpu.VMEM)
    return pl.pallas_call(
        functools.partial(rim_rows_body, tile=tile),
        out_shape=[shape, shape],
        in_specs=[pl.BlockSpec(memory_space=pltpu.SMEM)] + [vmem] * 3,
        out_specs=[vmem, vmem],
        compiler_params=pltpu.CompilerParams(vmem_limit_bytes=8 << 20),
        name="rim_rows",
    )(wet, state, west, east)


def prepare_weights(inner_ref, inner_bias_ref, outer_ref, inner_wide_ref, outer_half_ref, layers):
    f32 = jnp.float32
    bf16 = jnp.bfloat16
    _, channels, hidden_dim = inner_ref.shape
    which = lax.broadcasted_iota(jnp.int32, (channels, hidden_dim), 0)
    for index in layers:
        inner_wide_ref[index, 0:channels, :] = inner_ref[index]
        rest = inner_bias_ref[index : index + 1]
        tail = jnp.zeros((channels, hidden_dim), f32)
        for k in range(3):
            part = rest.astype(bf16).astype(f32)
            rest = rest - part
            tail = jnp.where(which == k, part, tail)
        inner_wide_ref[index, channels : 2 * channels, :] = tail.astype(bf16)
        outer_half_ref[index] = (outer_ref[index].astype(f32) * 0.5).astype(bf16)


def prepare_moments(average_ref, center_ref, channels):
    row = lax.broadcasted_iota(jnp.int32, (WIDE, WIDE), 0)
    col = lax.broadcasted_iota(jnp.int32, (WIDE, WIDE), 1)
    share = jnp.where(row // channels == col // channels, 1.0 / channels, 0.0)
    average_ref[...] = share.astype(jnp.bfloat16)
    center_ref[...] = (jnp.where(row == col, 1.0, 0.0) - share).astype(jnp.bfloat16)


def fill_wide(wide_ref, wet_ref, state_ref, west_ref, east_ref, rows, at, tile):
    f32 = jnp.float32
    _, width, _ = state_ref.shape
    first, last = rows
    here = slice(at, at + last - first)
    wide_ref[here, LEFT - RIM : LEFT, :] = west_ref[first:last, 0:RIM, :].astype(f32)
    wide_ref[here, LEFT + width : LEFT + width + RIM, :] = east_ref[first:last, 0:RIM, :].astype(f32)

    def widen(k, carry):
        for tj in range(width // tile):
            wet = wet_ref[(first + k) // tile, tj] > 0
            piece = state_ref[first + k, tj * tile : (tj + 1) * tile, :].astype(f32)
            wide_ref[at + k, LEFT + tj * tile : LEFT + (tj + 1) * tile, :] = jnp.where(
                wet, piece, 0.0
            )
        return carry

    lax.fori_loop(0, last - first, widen, 0, unroll=4)


def fill_mask(mask_ref, wets_ref, region, steps):
    for t in range(steps):
        wets_ref[region, t] = mask_ref[region, pl.ds(LEFT - REACH + t, STRIPS, stride=steps), :]


def fill_inner_masks(mask_ref, wets_ref, wet_ref, west_ref, east_ref, width, steps, tile):
    f32 = jnp.float32
    tiles_i, tiles_j = wet_ref.shape
    channels = west_ref.shape[2]
    for region in range(1, tiles_i + 1):
        for tj in range(tiles_j):
            flag = jnp.where(wet_ref[region - 1, tj] > 0, 1.0, 0.0)
            mask_ref[region, LEFT + tj * tile : LEFT + (tj + 1) * tile, :] = jnp.full(
                (tile, channels), flag, f32
            )
        edge = (region - 1) * tile
        for side_ref, at in ((west_ref, LEFT - REACH), (east_ref, LEFT + width)):
            mask_ref[region, at : at + REACH, :] = jnp.broadcast_to(
                side_ref[edge, RIM : RIM + 1, :].astype(f32), (REACH, channels)
            )
        fill_mask(mask_ref, wets_ref, region, steps)


def run_layer(
    index,
    source_ref,
    band_ref,
    start,
    steps,
    sources,
    picks,
    weights,
    packed,
    store,
    finish=None,
):
    gain_ref, bias_ref, outer_bias_ref, inner_wide_ref, outer_half_ref, average_ref, center_ref = weights
    phased_ref, grouped_ref, cells_ref, normed_ref = packed
    bf16 = jnp.bfloat16
    f32 = jnp.float32
    channels = gain_ref.shape[1]
    groups = channels // SEG
    pairs = steps // PHASE_J
    blocks = sum(n for _, n in picks[0])
    count = PHASE_I * pairs * STRIPS
    gain = jnp.concatenate([gain_ref[index : index + 1]] * 2, axis=1)
    shift = jnp.concatenate([bias_ref[index : index + 1]] * 2, axis=1)
    bias_lanes = jnp.where(
        lax.broadcasted_iota(jnp.int32, (count, channels), 1) < 3, 1.0, 0.0
    ).astype(bf16)

    def to_phases(blk, carry):
        for u in range(pairs + 3):
            for half in range(2):
                parts = []
                for p in range(8):
                    pi, pj = (half * 8 + p) // 2, (half * 8 + p) % 2
                    strip = source_ref[
                        blk * PHASE_I + pi, pl.ds(start + 2 * u + pj, STRIPS, stride=steps), :
                    ]
                    parts.append(strip.astype(bf16))
                for g, part in enumerate(swap_segments(parts)):
                    phased_ref[g, half, blk, u] = part
        return carry

    lax.fori_loop(0, sources, to_phases, 0)

    def convolve(g, carry):
        slabs = []
        mats = []
        for kb in range(2):
            for ub in range(4):
                for half in range(2):
                    runs = [
                        phased_ref[g, half, first : first + n, ub : ub + pairs].reshape(
                            n * pairs * STRIPS, LANES
                        )
                        for first, n in picks[kb]
                    ]
                    slabs.append(runs[0] if len(runs) == 1 else jnp.concatenate(runs, axis=0))
                band = band_ref.at[g, kb * 4 + ub]
                mats.append(jnp.concatenate([band[0], band[1]], axis=1))
        total = jnp.dot(
            jnp.concatenate(slabs, axis=1),
            jnp.concatenate(mats, axis=0),
            preferred_element_type=f32,
        ).astype(bf16)
        for half in range(2):
            grouped_ref[g, half, 0:blocks, 0:pairs] = total[
                :, half * LANES : (half + 1) * LANES
            ].reshape(blocks, pairs, STRIPS, LANES)
        return carry

    lax.fori_loop(0, groups, convolve, 0, unroll=4)

    def to_cells(blk):
        for v in range(pairs):
            for half in range(2):
                parts = swap_segments(
                    [grouped_ref[g, half, blk, v] for g in range(groups)], back=True
                )
                for p in range(8):
                    pi, pj = (half * 8 + p) // 2, (half * 8 + p) % 2
                    cells_ref[pj, pi, v] = parts[p]

    def normalize():
        conv = jnp.concatenate(
            [cells_ref[pj, :, 0:pairs].reshape(count, channels) for pj in range(PHASE_J)],
            axis=1,
        )
        centered = jnp.dot(conv, center_ref[...], preferred_element_type=f32)
        var = jnp.dot(
            (centered * centered).astype(bf16), average_ref[...], preferred_element_type=f32
        )
        normed = (centered * lax.rsqrt(var + 1e-06) * gain + shift).astype(bf16)
        for pj in range(PHASE_J):
            normed_ref[pj, 0:count] = normed[:, pj * channels : (pj + 1) * channels]

    def mix(blk, carry):
        if finish is not None:
            finish(jnp.maximum(blk - 1, 0))
        for pj in range(PHASE_J):
            pre = jnp.dot(
                jnp.concatenate([normed_ref[pj, 0:count], bias_lanes], axis=1),
                inner_wide_ref[index],
                preferred_element_type=f32,
            )
            hidden = (pre * (1.0 + lax.erf(pre * 0.7071067811865476))).astype(bf16)
            branch = (
                jnp.dot(hidden, outer_half_ref[index], preferred_element_type=f32)
                + outer_bias_ref[index : index + 1]
            ).reshape(PHASE_I, pairs, STRIPS, channels)
            for pi in range(PHASE_I):
                for v in range(pairs):
                    store(blk, pi, 2 * v + pj, branch[pi, v])
        normalize()
        to_cells(jnp.minimum(blk + 2, blocks - 1))
        return carry

    to_cells(0)
    normalize()
    to_cells(1)
    lax.fori_loop(0, blocks, mix, 0)
    if finish is not None:
        finish(blocks - 1)


def region_of(r, height, tile):
    region = jnp.int32(0)
    for bound in range(REACH, REACH + height + 1, tile):
        region += (r >= bound).astype(jnp.int32)
    return region


def inner_body(
    wet_ref,
    state_ref,
    west_ref,
    east_ref,
    band_ref,
    gain_ref,
    bias_ref,
    inner_ref,
    inner_bias_ref,
    outer_ref,
    outer_bias_ref,
    out_ref,
    wide_ref,
    mask_ref,
    wets_ref,
    average_ref,
    center_ref,
    inner_wide_ref,
    outer_half_ref,
    *,
    tile,
    steps,
    **packed,
):
    height, width, channels = state_ref.shape
    blocks = out_ref.shape[0] // PHASE_I
    f32 = jnp.float32
    top = PHASE_I - RIM
    wide_ref[:, LEFT + width :, :] = jnp.zeros(
        (wide_ref.shape[0], wide_ref.shape[1] - LEFT - width, channels), f32
    )
    fill_wide(
        wide_ref, wet_ref, state_ref, west_ref, east_ref, (top, top + wide_ref.shape[0]), 0, tile
    )
    mask_ref[...] = jnp.zeros(mask_ref.shape, f32)
    fill_inner_masks(mask_ref, wets_ref, wet_ref, west_ref, east_ref, width, steps, tile)
    prepare_weights(inner_ref, inner_bias_ref, outer_ref, inner_wide_ref, outer_half_ref, (0,))
    prepare_moments(average_ref, center_ref, channels)

    def store(blk, pi, t, branch):
        k = blk * PHASE_I + pi
        at = pl.ds(LEFT - REACH + t, STRIPS, stride=steps)
        region = region_of(k + PHASE_I, height, tile)
        out_ref[k, at, :] = (wide_ref[k + REACH, at, :] + branch) * wets_ref[region, t]

    run_layer(
        0,
        wide_ref,
        band_ref,
        LEFT - RIM,
        steps,
        blocks + 1,
        [[(kb, blocks)] for kb in range(2)],
        (gain_ref, bias_ref, outer_bias_ref, inner_wide_ref, outer_half_ref, average_ref, center_ref),
        tuple(packed[k] for k in PACKED),
        store,
    )


def outer_body(
    wet_ref,
    state_ref,
    top_ref,
    bottom_ref,
    west_ref,
    east_ref,
    band_a_ref,
    band_b_ref,
    part_ref,
    gain_ref,
    bias_ref,
    inner_ref,
    inner_bias_ref,
    outer_ref,
    outer_bias_ref,
    out_ref,
    wide_ref,
    second_ref,
    mask_ref,
    wets_ref,
    branch_ref,
    average_ref,
    center_ref,
    inner_wide_ref,
    outer_half_ref,
    sem,
    *,
    tile,
    steps,
    **packed,
):
    height, width, channels = state_ref.shape
    bf16 = jnp.bfloat16
    f32 = jnp.float32
    inner_rows = part_ref.shape[0]
    low = PHASE_I + inner_rows
    copy = pltpu.make_async_copy(part_ref, second_ref.at[PHASE_I:low], sem)
    copy.start()

    cut = 2 * PHASE_I
    ends = cut + height + RIM - low
    wide_ref[:, LEFT + width :, :] = jnp.zeros(
        (wide_ref.shape[0], wide_ref.shape[1] - LEFT - width, channels), f32
    )
    wide_ref[ends + RIM :] = jnp.zeros((wide_ref.shape[0] - ends - RIM,) + wide_ref.shape[1:], f32)
    span = slice(0, width + 2 * LEFT)
    wide_ref[0:RIM, span, :] = top_ref[0:RIM].astype(f32)
    wide_ref[ends : ends + RIM, span, :] = bottom_ref[0:RIM].astype(f32)
    fill_wide(wide_ref, wet_ref, state_ref, west_ref, east_ref, (0, cut - RIM), RIM, tile)
    fill_wide(wide_ref, wet_ref, state_ref, west_ref, east_ref, (low - RIM, height), cut, tile)
    mask_ref[...] = jnp.zeros(mask_ref.shape, f32)
    fill_inner_masks(mask_ref, wets_ref, wet_ref, west_ref, east_ref, width, steps, tile)
    for region, rim_ref in ((0, top_ref), (mask_ref.shape[0] - 1, bottom_ref)):
        mask_ref[region, span, :] = rim_ref[RIM].astype(f32)
        fill_mask(mask_ref, wets_ref, region, steps)
    prepare_weights(inner_ref, inner_bias_ref, outer_ref, inner_wide_ref, outer_half_ref, (0, 1))
    prepare_moments(average_ref, center_ref, channels)
    weights = (
        gain_ref,
        bias_ref,
        outer_bias_ref,
        inner_wide_ref,
        outer_half_ref,
        average_ref,
        center_ref,
    )
    packed = tuple(packed[k] for k in PACKED)

    def store_first(blk, pi, t, branch):
        later = (blk > 0).astype(jnp.int32)
        r = blk * PHASE_I + pi + later * inner_rows
        at = pl.ds(LEFT - REACH + t, STRIPS, stride=steps)
        base = wide_ref[(blk + later) * PHASE_I + pi + REACH, at, :]
        second_ref[r, at, :] = (base + branch) * wets_ref[region_of(r, height, tile), t]

    tails = wide_ref.shape[0] // PHASE_I - 3
    run_layer(
        0,
        wide_ref,
        band_a_ref,
        LEFT - RIM,
        steps,
        tails + 3,
        [[(kb, 1), (2 + kb, tails)] for kb in range(2)],
        weights,
        packed,
        store_first,
    )
    copy.wait()
    steps_b = width // STRIPS
    blocks = height // PHASE_I

    def store_second(blk, pi, t, branch):
        branch_ref[pi, t * STRIPS : (t + 1) * STRIPS, :] = branch

    def finish(blk):
        for pi in range(PHASE_I):
            i = blk * PHASE_I + pi
            for s in range(0, STRIPS, 2):
                wet = wet_ref[i // tile, s * steps_b // tile] > 0
                delta = jnp.concatenate(
                    [branch_ref[pi, pl.ds(s + k, steps_b, stride=STRIPS), :] for k in range(2)],
                    axis=0,
                )
                base = second_ref[i + REACH, LEFT + s * steps_b : LEFT + (s + 2) * steps_b, :]
                out_ref[i, s * steps_b : (s + 2) * steps_b, :] = jnp.where(
                    wet, base + delta, 0.0
                ).astype(bf16)

    run_layer(
        1,
        second_ref,
        band_b_ref,
        LEFT - REACH,
        steps_b,
        blocks + 1,
        [[(kb, blocks)] for kb in range(2)],
        weights,
        packed,
        store_second,
        finish,
    )


PACKED = ("phased_ref", "grouped_ref", "cells_ref", "normed_ref")


def in_kernel(body, groups, sources, blocks, pairs, **options):
    packed = dict(
        phased_ref=pltpu.VMEM((groups, 2, sources, pairs + 3, STRIPS, LANES), jnp.bfloat16),
        grouped_ref=pltpu.VMEM((groups, 2, blocks, pairs, STRIPS, LANES), jnp.bfloat16),
        cells_ref=pltpu.VMEM((PHASE_J, PHASE_I, pairs, STRIPS, LANES), jnp.bfloat16),
        normed_ref=pltpu.VMEM((PHASE_J, PHASE_I * pairs * STRIPS, LANES), jnp.bfloat16),
    )

    def run(*refs):
        pl.run_scoped(functools.partial(body, *refs, **options), **packed)

    return run


def plan(state):
    height, width, channels = state.shape
    blocks = pl.cdiv(height + 2 * REACH, PHASE_I)
    steps = PHASE_J * pl.cdiv(width + 2 * REACH, STRIPS * PHASE_J)
    inner = (height + RIM - 2 * PHASE_I) // PHASE_I
    assert channels == LANES and width == STRIPS * 8 and height % PHASE_I == 0 and inner > 1
    return blocks, steps, inner


def shared_scratch(weights, regions, span, steps):
    channels, hidden = weights[2].shape[1:]
    return (
        [
            pltpu.VMEM((regions, span, channels), jnp.float32),
            pltpu.VMEM((regions, steps, STRIPS, channels), jnp.float32),
        ],
        [
            pltpu.VMEM((WIDE, WIDE), jnp.bfloat16),
            pltpu.VMEM((WIDE, WIDE), jnp.bfloat16),
            pltpu.VMEM((2, 2 * channels, hidden), jnp.bfloat16),
            pltpu.VMEM((2, hidden, channels), jnp.bfloat16),
        ],
    )


def inner_call(wet, state, west, east, band, weights, tile):
    height, _, channels = state.shape
    _, steps, inner = plan(state)
    span = LEFT + STRIPS * steps
    vmem = pl.BlockSpec(memory_space=pltpu.VMEM)
    masks, mats = shared_scratch(weights, height // tile + 2, span, steps)
    cells = PHASE_I * inner * STRIPS * steps
    return pl.pallas_call(
        in_kernel(
            inner_body, channels // SEG, inner + 1, inner, steps // PHASE_J, tile=tile, steps=steps
        ),
        out_shape=jax.ShapeDtypeStruct((PHASE_I * inner, span, channels), jnp.float32),
        in_specs=[pl.BlockSpec(memory_space=pltpu.SMEM)] + [vmem] * 10,
        out_specs=vmem,
        scratch_shapes=[pltpu.VMEM((PHASE_I * (inner + 1), span, channels), jnp.float32)]
        + masks
        + mats,
        compiler_params=pltpu.CompilerParams(vmem_limit_bytes=INNER_MIB << 20),
        cost_estimate=pl.CostEstimate(
            flops=cells * channels * 2000, bytes_accessed=cells * channels * 8, transcendentals=0
        ),
        name="inner_blocks",
    )(wet, state, west, east, band, *weights)


def outer_call(wet, state, top, bottom, west, east, bands, part, weights, tile):
    height, width, channels = state.shape
    blocks, steps, inner = plan(state)
    span = LEFT + STRIPS * steps
    vmem = pl.BlockSpec(memory_space=pltpu.VMEM)
    masks, mats = shared_scratch(weights, height // tile + 2, span, steps)
    tails = blocks - 1 - inner
    return pl.pallas_call(
        in_kernel(
            outer_body,
            channels // SEG,
            height // PHASE_I + 1,
            height // PHASE_I,
            steps // PHASE_J,
            tile=tile,
            steps=steps,
        ),
        out_shape=jax.ShapeDtypeStruct(state.shape, jnp.bfloat16),
        in_specs=[pl.BlockSpec(memory_space=pltpu.SMEM)] + [vmem] * 14,
        out_specs=vmem,
        scratch_shapes=[
            pltpu.VMEM((PHASE_I * (tails + 3), span, channels), jnp.float32),
            pltpu.VMEM((PHASE_I * blocks, span, channels), jnp.float32),
        ]
        + masks
        + [pltpu.VMEM((PHASE_I, width, channels), jnp.float32)]
        + mats
        + [pltpu.SemaphoreType.DMA],
        compiler_params=pltpu.CompilerParams(vmem_limit_bytes=OUTER_MIB << 20),
        name="outer_blocks",
    )(wet, state, top, bottom, west, east, *bands, part, *weights)


def shift_pair(head, tail, axis, closed):
    count = lax.axis_size(axis)
    ends = count if closed else count - 1
    before = lax.ppermute(tail, axis, [(i, (i + 1) % count) for i in range(ends)])
    after = lax.ppermute(head, axis, [((i + 1) % count, i) for i in range(ends)])
    return before, after


def per_device(
    ocean_field,
    wet_tiles,
    conv_weight,
    norm_gain,
    norm_bias,
    inner_weight,
    inner_bias,
    outer_weight,
    outer_bias,
):
    tile = ocean_field.shape[0] // wet_tiles.shape[0]
    cols = rim_cols_call(wet_tiles, ocean_field, tile)
    west, east = shift_pair(*cols, "lat", False)
    rows = rim_rows_call(wet_tiles, ocean_field, west, east, tile)
    top, bottom = shift_pair(*rows, "lon", True)
    bands = []
    for layer in range(conv_weight.shape[0]):
        bands.append(band_call(conv_weight, layer))
    weights = (norm_gain, norm_bias, inner_weight, inner_bias, outer_weight, outer_bias)
    part = inner_call(wet_tiles, ocean_field, west, east, bands[0], weights, tile)
    return outer_call(wet_tiles, ocean_field, top, bottom, west, east, bands, part, weights, tile)


def solution(mesh):
    return jax.shard_map(
        per_device,
        mesh=mesh,
        in_specs=(P("lon", "lat", None), P("lon", "lat"), P(), P(), P(), P(), P(), P(), P()),
        out_specs=P("lon", "lat", None),
        check_vma=False,
    )
```

```python
import functools

import jax
import jax.numpy as jnp
from jax import lax
from jax.experimental import pallas as pl
from jax.experimental.pallas import tpu as pltpu
from jax.sharding import PartitionSpec as P

PHASE_I = 8
PHASE_J = 2
PHASES = PHASE_I * PHASE_J
SEG = 16
STRIPS = 16
LEFT = 8
REACH = 3
RIM = 2 * REACH
LANES = 128
WIDE = 256
CHUNKS = 8
INNER_MIB = 20
OUTER_MIB = 26
WHOLE_VMEM = 67043328


def swap_segments(parts, back=False):
    parts = list(parts)
    lane = lax.broadcasted_iota(jnp.int32, parts[0].shape, 1)
    for dist in (1, 2, 4) if back else (4, 2, 1):
        low_side = (lane // (SEG * dist)) % 2 == 0
        turn = LANES - SEG * dist if back else SEG * dist
        for p in range(8):
            if p & dist:
                continue
            low, high = parts[p], parts[p + dist]
            moved = pltpu.roll(jnp.where(low_side, high, low), turn, 1)
            parts[p] = jnp.where(low_side, low, moved)
            parts[p + dist] = jnp.where(low_side, moved, high)
    return parts


def lane_slot(g, p):
    p1, p2, p4 = p & 1, p >> 1 & 1, p >> 2 & 1
    high = p4 ^ ((g >> 1) & (1 - p2))
    return ((high * 2 + p2 + (g & (1 - p1))) & 3) * 2 + p1


def band_body(conv_ref, band_ref, taps_ref, rows_ref, *, layer):
    f32 = jnp.float32
    g = pl.program_id(0)

    @pl.when(g == 0)
    def _():
        taps_ref[...] = jnp.zeros(taps_ref.shape, f32)
        taps_ref[7:14, 8:15, :] = conv_ref[:, :, layer, :].astype(f32)

        def tap_rows(q, carry):
            for half in range(2):
                parts = []
                for p in range(8):
                    pi, pj = (half * 8 + p) // 2, (half * 8 + p) % 2
                    parts.append(taps_ref[q - pi + 7, pl.ds(8 - pj, 8), :])
                for group, part in enumerate(swap_segments(parts)):
                    rows_ref[group, q, half] = part
            return carry

        lax.fori_loop(0, 2 * PHASE_I, tap_rows, 0, unroll=4)

    lane = lax.broadcasted_iota(jnp.int32, (SEG, LANES), 1)
    own = lax.broadcasted_iota(jnp.int32, (SEG, LANES), 0) == lane % SEG
    for kb in range(2):
        for p in range(PHASES):
            slot = (p >> 3) * 8 + lane_slot(g, p & 7)
            at = pl.ds(pl.multiple_of(slot * SEG, SEG), SEG)
            for ub in range(4):
                r = 2 * ub + (p & 1)
                for half in range(2):
                    row = rows_ref[g, kb * PHASE_I + (p >> 1), half, r : r + 1, :]
                    band_ref[0, kb * 4 + ub, half, at, :] = jnp.where(
                        own, jnp.broadcast_to(row, (SEG, LANES)), 0.0
                    ).astype(jnp.bfloat16)


def band_call(kernels, layer):
    groups = kernels.shape[3] // SEG
    return pl.pallas_call(
        functools.partial(band_body, layer=layer),
        grid=(groups,),
        out_shape=jax.ShapeDtypeStruct((groups, CHUNKS, 2, WIDE, LANES), jnp.bfloat16),
        in_specs=[pl.BlockSpec(kernels.shape, lambda g: (0, 0, 0, 0))],
        out_specs=pl.BlockSpec((1, CHUNKS, 2, WIDE, LANES), lambda g: (g, 0, 0, 0, 0)),
        scratch_shapes=[
            pltpu.VMEM((24, 24, LANES), jnp.float32),
            pltpu.VMEM((groups, 2 * PHASE_I, 2, 8, LANES), jnp.float32),
        ],
        compiler_params=pltpu.CompilerParams(vmem_limit_bytes=16 << 20),
        cost_estimate=pl.CostEstimate(
            flops=16 << 20, bytes_accessed=groups * CHUNKS * WIDE * WIDE * 2, transcendentals=0
        ),
        name="bands",
    )(kernels)


def rim_cols_body(wet_hbm, state_hbm, head_ref, tail_ref, wet_ref, left_ref, right_ref, sems, *, tile):
    f32 = jnp.float32
    _, chunk, channels = left_ref.shape
    width = state_hbm.shape[1]
    copies = [
        pltpu.make_async_copy(wet_hbm, wet_ref, sems.at[0]),
        pltpu.make_async_copy(state_hbm.at[:, 0:chunk, :], left_ref, sems.at[1]),
        pltpu.make_async_copy(state_hbm.at[:, width - chunk : width, :], right_ref, sems.at[2]),
    ]
    for copy in copies:
        copy.start()
    for copy in copies:
        copy.wait()
    tiles_i, tiles_j = wet_ref.shape
    for cols_ref, out_ref, tj, first in (
        (left_ref, head_ref, 0, 0),
        (right_ref, tail_ref, tiles_j - 1, chunk - RIM),
    ):
        for ti in range(tiles_i):
            wet = wet_ref[ti, tj] > 0
            at = slice(ti * tile, (ti + 1) * tile)
            piece = cols_ref[at].astype(f32)
            kept = jnp.where(wet, piece[:, first : first + RIM], 0.0)
            flag = jnp.full((tile, 1, channels), jnp.where(wet, 1.0, 0.0), f32)
            out_ref[at] = jnp.concatenate([kept, flag], axis=1).astype(jnp.bfloat16)


def rim_cols_call(wet, state, tile):
    height, _, channels = state.shape
    shape = jax.ShapeDtypeStruct((height, RIM + 1, channels), jnp.bfloat16)
    vmem = pl.BlockSpec(memory_space=pltpu.VMEM)
    hbm = pl.BlockSpec(memory_space=pltpu.HBM)
    return pl.pallas_call(
        functools.partial(rim_cols_body, tile=tile),
        out_shape=[shape, shape],
        in_specs=[hbm, hbm],
        out_specs=[vmem, vmem],
        scratch_shapes=[
            pltpu.SMEM(wet.shape, jnp.int32),
            pltpu.VMEM((height, 8, channels), state.dtype),
            pltpu.VMEM((height, 8, channels), state.dtype),
            pltpu.SemaphoreType.DMA((3,)),
        ],
        compiler_params=pltpu.CompilerParams(vmem_limit_bytes=WHOLE_VMEM),
        name="rim_cols",
    )(wet, state)


def rim_rows_body(
    wet_ref,
    state_ref,
    west_in_ref,
    east_in_ref,
    head_ref,
    tail_ref,
    west_ref,
    east_ref,
    *,
    tile,
):
    f32 = jnp.float32
    bf16 = jnp.bfloat16
    place = lax.axis_index("lat")
    for in_ref, clean_ref, inside in (
        (west_in_ref, west_ref, place > 0),
        (east_in_ref, east_ref, place < lax.axis_size("lat") - 1),
    ):
        clean_ref[...] = jnp.where(inside, in_ref[...].astype(f32), 0.0).astype(bf16)
    height, width, channels = state_ref.shape
    for out_ref, ti, first in ((head_ref, 0, 0), (tail_ref, wet_ref.shape[0] - 1, height - RIM)):
        out_ref[:, 0:LEFT, :] = jnp.zeros((RIM + 1, LEFT, channels), bf16)
        out_ref[:, LEFT + width :, :] = jnp.zeros((RIM + 1, LEFT, channels), bf16)
        for side_ref, at in ((west_ref, LEFT - RIM), (east_ref, LEFT + width)):
            side = side_ref[first : first + RIM].astype(f32)
            out_ref[0:RIM, at : at + RIM, :] = side[:, 0:RIM].astype(bf16)
            out_ref[RIM, at : at + RIM, :] = jnp.broadcast_to(
                side[0, RIM : RIM + 1], (RIM, channels)
            ).astype(bf16)
        for tj in range(width // tile):
            wet = wet_ref[ti, tj] > 0
            at = slice(LEFT + tj * tile, LEFT + (tj + 1) * tile)
            for r in range(RIM):
                piece = state_ref[first + r, tj * tile : (tj + 1) * tile, :].astype(f32)
                out_ref[r, at, :] = jnp.where(wet, piece, 0.0).astype(bf16)
            out_ref[RIM, at, :] = jnp.full(
                (tile, channels), jnp.where(wet, 1.0, 0.0), f32
            ).astype(bf16)


def rim_rows_call(wet, state, west, east, tile):
    _, width, channels = state.shape
    shape = jax.ShapeDtypeStruct((RIM + 1, width + 2 * LEFT, channels), jnp.bfloat16)
    vmem = pl.BlockSpec(memory_space=pltpu.VMEM)
    return pl.pallas_call(
        functools.partial(rim_rows_body, tile=tile),
        out_shape=[shape, shape] + [jax.ShapeDtypeStruct(west.shape, west.dtype)] * 2,
        in_specs=[pl.BlockSpec(memory_space=pltpu.SMEM)] + [vmem] * 3,
        out_specs=[vmem] * 4,
        compiler_params=pltpu.CompilerParams(vmem_limit_bytes=8 << 20),
        name="rim_rows",
    )(wet, state, west, east)


def prepare_weights(inner_ref, inner_bias_ref, outer_ref, inner_wide_ref, outer_half_ref, layers):
    f32 = jnp.float32
    bf16 = jnp.bfloat16
    _, channels, hidden_dim = inner_ref.shape
    which = lax.broadcasted_iota(jnp.int32, (channels, hidden_dim), 0)
    for index in layers:
        inner_wide_ref[index, 0:channels, :] = inner_ref[index]
        rest = inner_bias_ref[index : index + 1]
        tail = jnp.zeros((channels, hidden_dim), f32)
        for k in range(3):
            part = rest.astype(bf16).astype(f32)
            rest = rest - part
            tail = jnp.where(which == k, part, tail)
        inner_wide_ref[index, channels : 2 * channels, :] = tail.astype(bf16)
        outer_half_ref[index] = (outer_ref[index].astype(f32) * 0.5).astype(bf16)


def prepare_moments(average_ref, center_ref, channels):
    row = lax.broadcasted_iota(jnp.int32, (WIDE, WIDE), 0)
    col = lax.broadcasted_iota(jnp.int32, (WIDE, WIDE), 1)
    share = jnp.where(row // channels == col // channels, 1.0 / channels, 0.0)
    average_ref[...] = share.astype(jnp.bfloat16)
    center_ref[...] = (jnp.where(row == col, 1.0, 0.0) - share).astype(jnp.bfloat16)


def fill_wide(wide_ref, wet_ref, state_ref, west_ref, east_ref, rows, at, tile):
    f32 = jnp.float32
    _, width, _ = state_ref.shape
    first, last = rows
    here = slice(at, at + last - first)
    wide_ref[here, LEFT - RIM : LEFT, :] = west_ref[first:last, 0:RIM, :].astype(f32)
    wide_ref[here, LEFT + width : LEFT + width + RIM, :] = east_ref[first:last, 0:RIM, :].astype(f32)

    def widen(k, carry):
        for tj in range(width // tile):
            wet = wet_ref[(first + k) // tile, tj] > 0
            piece = state_ref[first + k, tj * tile : (tj + 1) * tile, :].astype(f32)
            wide_ref[at + k, LEFT + tj * tile : LEFT + (tj + 1) * tile, :] = jnp.where(
                wet, piece, 0.0
            )
        return carry

    lax.fori_loop(0, last - first, widen, 0, unroll=4)


def fill_mask(mask_ref, wets_ref, region, steps):
    for t in range(steps):
        wets_ref[region, t] = mask_ref[region, pl.ds(LEFT - REACH + t, STRIPS, stride=steps), :]


def fill_inner_masks(mask_ref, wets_ref, wet_ref, west_ref, east_ref, width, steps, tile):
    f32 = jnp.float32
    tiles_i, tiles_j = wet_ref.shape
    channels = west_ref.shape[2]
    for region in range(1, tiles_i + 1):
        for tj in range(tiles_j):
            flag = jnp.where(wet_ref[region - 1, tj] > 0, 1.0, 0.0)
            mask_ref[region, LEFT + tj * tile : LEFT + (tj + 1) * tile, :] = jnp.full(
                (tile, channels), flag, f32
            )
        edge = (region - 1) * tile
        for side_ref, at in ((west_ref, LEFT - REACH), (east_ref, LEFT + width)):
            mask_ref[region, at : at + REACH, :] = jnp.broadcast_to(
                side_ref[edge, RIM : RIM + 1, :].astype(f32), (REACH, channels)
            )
        fill_mask(mask_ref, wets_ref, region, steps)


def run_layer(
    index,
    source_ref,
    band_ref,
    start,
    steps,
    sources,
    picks,
    weights,
    packed,
    store,
    finish=None,
):
    gain_ref, bias_ref, outer_bias_ref, inner_wide_ref, outer_half_ref, average_ref, center_ref = weights
    phased_ref, grouped_ref, cells_ref, normed_ref = packed
    bf16 = jnp.bfloat16
    f32 = jnp.float32
    channels = gain_ref.shape[1]
    groups = channels // SEG
    pairs = steps // PHASE_J
    blocks = sum(n for _, n in picks[0])
    count = PHASE_I * pairs * STRIPS
    gain = jnp.concatenate([gain_ref[index : index + 1]] * 2, axis=1)
    shift = jnp.concatenate([bias_ref[index : index + 1]] * 2, axis=1)
    bias_lanes = jnp.where(
        lax.broadcasted_iota(jnp.int32, (count, channels), 1) < 3, 1.0, 0.0
    ).astype(bf16)

    def to_phases(blk, carry):
        for u in range(pairs + 3):
            for half in range(2):
                parts = []
                for p in range(8):
                    pi, pj = (half * 8 + p) // 2, (half * 8 + p) % 2
                    strip = source_ref[
                        blk * PHASE_I + pi, pl.ds(start + 2 * u + pj, STRIPS, stride=steps), :
                    ]
                    parts.append(strip.astype(bf16))
                for g, part in enumerate(swap_segments(parts)):
                    phased_ref[g, half, blk, u] = part
        return carry

    lax.fori_loop(0, sources, to_phases, 0)

    def convolve(g, carry):
        slabs = []
        mats = []
        for kb in range(2):
            for ub in range(4):
                for half in range(2):
                    runs = [
                        phased_ref[g, half, first : first + n, ub : ub + pairs].reshape(
                            n * pairs * STRIPS, LANES
                        )
                        for first, n in picks[kb]
                    ]
                    slabs.append(runs[0] if len(runs) == 1 else jnp.concatenate(runs, axis=0))
                band = band_ref.at[g, kb * 4 + ub]
                mats.append(jnp.concatenate([band[0], band[1]], axis=1))
        total = jnp.dot(
            jnp.concatenate(slabs, axis=1),
            jnp.concatenate(mats, axis=0),
            preferred_element_type=f32,
        ).astype(bf16)
        for half in range(2):
            grouped_ref[g, half, 0:blocks, 0:pairs] = total[
                :, half * LANES : (half + 1) * LANES
            ].reshape(blocks, pairs, STRIPS, LANES)
        return carry

    lax.fori_loop(0, groups, convolve, 0, unroll=8)

    def to_cells(blk):
        for v in range(pairs):
            for half in range(2):
                parts = swap_segments(
                    [grouped_ref[g, half, blk, v] for g in range(groups)], back=True
                )
                for p in range(8):
                    pi, pj = (half * 8 + p) // 2, (half * 8 + p) % 2
                    cells_ref[pj, pi, v] = parts[p]

    def normalize():
        conv = jnp.concatenate(
            [cells_ref[pj, :, 0:pairs].reshape(count, channels) for pj in range(PHASE_J)],
            axis=1,
        )
        centered = jnp.dot(conv, center_ref[...], preferred_element_type=f32)
        var = jnp.dot(
            (centered * centered).astype(bf16), average_ref[...], preferred_element_type=f32
        )
        normed = (centered * lax.rsqrt(var + 1e-06) * gain + shift).astype(bf16)
        for pj in range(PHASE_J):
            normed_ref[pj, 0:count] = normed[:, pj * channels : (pj + 1) * channels]

    def mix(blk, carry):
        if finish is not None:
            finish(jnp.maximum(blk - 1, 0))
        for pj in range(PHASE_J):
            pre = jnp.dot(
                jnp.concatenate([normed_ref[pj, 0:count], bias_lanes], axis=1),
                inner_wide_ref[index],
                preferred_element_type=f32,
            )
            hidden = (pre * (1.0 + lax.erf(pre * 0.7071067811865476))).astype(bf16)
            branch = (
                jnp.dot(hidden, outer_half_ref[index], preferred_element_type=f32)
                + outer_bias_ref[index : index + 1]
            ).reshape(PHASE_I, pairs, STRIPS, channels)
            for pi in range(PHASE_I):
                for v in range(pairs):
                    store(blk, pi, 2 * v + pj, branch[pi, v])
        normalize()
        to_cells(jnp.minimum(blk + 2, blocks - 1))
        return carry

    to_cells(0)
    normalize()
    to_cells(1)
    lax.fori_loop(0, blocks, mix, 0, unroll=2)
    if finish is not None:
        finish(blocks - 1)


def region_of(r, height, tile):
    region = jnp.int32(0)
    for bound in range(REACH, REACH + height + 1, tile):
        region += (r >= bound).astype(jnp.int32)
    return region


def inner_body(
    wet_ref,
    state_ref,
    west_ref,
    east_ref,
    band_ref,
    gain_ref,
    bias_ref,
    inner_ref,
    inner_bias_ref,
    outer_ref,
    outer_bias_ref,
    out_ref,
    wide_ref,
    mask_ref,
    wets_ref,
    average_ref,
    center_ref,
    inner_wide_ref,
    outer_half_ref,
    *,
    tile,
    steps,
    **packed,
):
    height, width, channels = state_ref.shape
    blocks = out_ref.shape[0] // PHASE_I
    f32 = jnp.float32
    top = PHASE_I - RIM
    wide_ref[:, LEFT + width :, :] = jnp.zeros(
        (wide_ref.shape[0], wide_ref.shape[1] - LEFT - width, channels), f32
    )
    fill_wide(
        wide_ref, wet_ref, state_ref, west_ref, east_ref, (top, top + wide_ref.shape[0]), 0, tile
    )
    mask_ref[...] = jnp.zeros(mask_ref.shape, f32)
    fill_inner_masks(mask_ref, wets_ref, wet_ref, west_ref, east_ref, width, steps, tile)
    prepare_weights(inner_ref, inner_bias_ref, outer_ref, inner_wide_ref, outer_half_ref, (0,))
    prepare_moments(average_ref, center_ref, channels)

    def store(blk, pi, t, branch):
        k = blk * PHASE_I + pi
        at = pl.ds(LEFT - REACH + t, STRIPS, stride=steps)
        region = region_of(k + PHASE_I, height, tile)
        out_ref[k, at, :] = (wide_ref[k + REACH, at, :] + branch) * wets_ref[region, t]

    run_layer(
        0,
        wide_ref,
        band_ref,
        LEFT - RIM,
        steps,
        blocks + 1,
        [[(kb, blocks)] for kb in range(2)],
        (gain_ref, bias_ref, outer_bias_ref, inner_wide_ref, outer_half_ref, average_ref, center_ref),
        tuple(packed[k] for k in PACKED),
        store,
    )


def outer_body(
    wet_ref,
    state_ref,
    top_ref,
    bottom_ref,
    west_ref,
    east_ref,
    band_a_ref,
    band_b_ref,
    part_ref,
    gain_ref,
    bias_ref,
    inner_ref,
    inner_bias_ref,
    outer_ref,
    outer_bias_ref,
    out_ref,
    wide_ref,
    second_ref,
    mask_ref,
    wets_ref,
    branch_ref,
    average_ref,
    center_ref,
    inner_wide_ref,
    outer_half_ref,
    sem,
    *,
    tile,
    steps,
    **packed,
):
    height, width, channels = state_ref.shape
    bf16 = jnp.bfloat16
    f32 = jnp.float32
    inner_rows = part_ref.shape[0]
    low = PHASE_I + inner_rows
    copy = pltpu.make_async_copy(part_ref, second_ref.at[PHASE_I:low], sem)
    copy.start()

    cut = 2 * PHASE_I
    ends = cut + height + RIM - low
    wide_ref[:, LEFT + width :, :] = jnp.zeros(
        (wide_ref.shape[0], wide_ref.shape[1] - LEFT - width, channels), f32
    )
    wide_ref[ends + RIM :] = jnp.zeros((wide_ref.shape[0] - ends - RIM,) + wide_ref.shape[1:], f32)
    span = slice(0, width + 2 * LEFT)
    wide_ref[0:RIM, span, :] = top_ref[0:RIM].astype(f32)
    wide_ref[ends : ends + RIM, span, :] = bottom_ref[0:RIM].astype(f32)
    fill_wide(wide_ref, wet_ref, state_ref, west_ref, east_ref, (0, cut - RIM), RIM, tile)
    fill_wide(wide_ref, wet_ref, state_ref, west_ref, east_ref, (low - RIM, height), cut, tile)
    mask_ref[...] = jnp.zeros(mask_ref.shape, f32)
    fill_inner_masks(mask_ref, wets_ref, wet_ref, west_ref, east_ref, width, steps, tile)
    for region, rim_ref in ((0, top_ref), (mask_ref.shape[0] - 1, bottom_ref)):
        mask_ref[region, span, :] = rim_ref[RIM].astype(f32)
        fill_mask(mask_ref, wets_ref, region, steps)
    prepare_weights(inner_ref, inner_bias_ref, outer_ref, inner_wide_ref, outer_half_ref, (0, 1))
    prepare_moments(average_ref, center_ref, channels)
    weights = (
        gain_ref,
        bias_ref,
        outer_bias_ref,
        inner_wide_ref,
        outer_half_ref,
        average_ref,
        center_ref,
    )
    packed = tuple(packed[k] for k in PACKED)

    def store_first(blk, pi, t, branch):
        later = (blk > 0).astype(jnp.int32)
        r = blk * PHASE_I + pi + later * inner_rows
        at = pl.ds(LEFT - REACH + t, STRIPS, stride=steps)
        base = wide_ref[(blk + later) * PHASE_I + pi + REACH, at, :]
        second_ref[r, at, :] = (base + branch) * wets_ref[region_of(r, height, tile), t]

    tails = wide_ref.shape[0] // PHASE_I - 3
    run_layer(
        0,
        wide_ref,
        band_a_ref,
        LEFT - RIM,
        steps,
        tails + 3,
        [[(kb, 1), (2 + kb, tails)] for kb in range(2)],
        weights,
        packed,
        store_first,
    )
    copy.wait()
    steps_b = width // STRIPS
    blocks = height // PHASE_I

    def store_second(blk, pi, t, branch):
        branch_ref[pi, t * STRIPS : (t + 1) * STRIPS, :] = branch

    def finish(blk):
        for pi in range(PHASE_I):
            i = blk * PHASE_I + pi
            for s in range(0, STRIPS, 2):
                wet = wet_ref[i // tile, s * steps_b // tile] > 0
                delta = jnp.concatenate(
                    [branch_ref[pi, pl.ds(s + k, steps_b, stride=STRIPS), :] for k in range(2)],
                    axis=0,
                )
                base = second_ref[i + REACH, LEFT + s * steps_b : LEFT + (s + 2) * steps_b, :]
                out_ref[i, s * steps_b : (s + 2) * steps_b, :] = jnp.where(
                    wet, base + delta, 0.0
                ).astype(bf16)

    run_layer(
        1,
        second_ref,
        band_b_ref,
        LEFT - REACH,
        steps_b,
        blocks + 1,
        [[(kb, blocks)] for kb in range(2)],
        weights,
        packed,
        store_second,
        finish,
    )


PACKED = ("phased_ref", "grouped_ref", "cells_ref", "normed_ref")


def in_kernel(body, groups, sources, blocks, pairs, **options):
    packed = dict(
        phased_ref=pltpu.VMEM((groups, 2, sources, pairs + 3, STRIPS, LANES), jnp.bfloat16),
        grouped_ref=pltpu.VMEM((groups, 2, blocks, pairs, STRIPS, LANES), jnp.bfloat16),
        cells_ref=pltpu.VMEM((PHASE_J, PHASE_I, pairs, STRIPS, LANES), jnp.bfloat16),
        normed_ref=pltpu.VMEM((PHASE_J, PHASE_I * pairs * STRIPS, LANES), jnp.bfloat16),
    )

    def run(*refs):
        pl.run_scoped(functools.partial(body, *refs, **options), **packed)

    return run


def plan(state):
    height, width, channels = state.shape
    blocks = pl.cdiv(height + 2 * REACH, PHASE_I)
    steps = PHASE_J * pl.cdiv(width + 2 * REACH, STRIPS * PHASE_J)
    inner = (height + RIM - 2 * PHASE_I) // PHASE_I
    assert channels == LANES and width == STRIPS * 8 and height % PHASE_I == 0 and inner > 1
    return blocks, steps, inner


def shared_scratch(weights, regions, span, steps):
    channels, hidden = weights[2].shape[1:]
    return (
        [
            pltpu.VMEM((regions, span, channels), jnp.float32),
            pltpu.VMEM((regions, steps, STRIPS, channels), jnp.float32),
        ],
        [
            pltpu.VMEM((WIDE, WIDE), jnp.bfloat16),
            pltpu.VMEM((WIDE, WIDE), jnp.bfloat16),
            pltpu.VMEM((2, 2 * channels, hidden), jnp.bfloat16),
            pltpu.VMEM((2, hidden, channels), jnp.bfloat16),
        ],
    )


def inner_call(wet, state, west, east, band, weights, tile):
    height, _, channels = state.shape
    _, steps, inner = plan(state)
    span = LEFT + STRIPS * steps
    vmem = pl.BlockSpec(memory_space=pltpu.VMEM)
    masks, mats = shared_scratch(weights, height // tile + 2, span, steps)
    cells = PHASE_I * inner * STRIPS * steps
    return pl.pallas_call(
        in_kernel(
            inner_body, channels // SEG, inner + 1, inner, steps // PHASE_J, tile=tile, steps=steps
        ),
        out_shape=jax.ShapeDtypeStruct((PHASE_I * inner, span, channels), jnp.float32),
        in_specs=[pl.BlockSpec(memory_space=pltpu.SMEM)] + [vmem] * 10,
        out_specs=vmem,
        scratch_shapes=[pltpu.VMEM((PHASE_I * (inner + 1), span, channels), jnp.float32)]
        + masks
        + mats,
        compiler_params=pltpu.CompilerParams(vmem_limit_bytes=INNER_MIB << 20),
        cost_estimate=pl.CostEstimate(
            flops=cells * channels * 2000, bytes_accessed=cells * channels * 8, transcendentals=0
        ),
        name="inner_blocks",
    )(wet, state, west, east, band, *weights)


def outer_call(wet, state, top, bottom, west, east, bands, part, weights, tile):
    height, width, channels = state.shape
    blocks, steps, inner = plan(state)
    span = LEFT + STRIPS * steps
    vmem = pl.BlockSpec(memory_space=pltpu.VMEM)
    masks, mats = shared_scratch(weights, height // tile + 2, span, steps)
    tails = blocks - 1 - inner
    return pl.pallas_call(
        in_kernel(
            outer_body,
            channels // SEG,
            height // PHASE_I + 1,
            height // PHASE_I,
            steps // PHASE_J,
            tile=tile,
            steps=steps,
        ),
        out_shape=jax.ShapeDtypeStruct(state.shape, jnp.bfloat16),
        in_specs=[pl.BlockSpec(memory_space=pltpu.SMEM)] + [vmem] * 14,
        out_specs=vmem,
        scratch_shapes=[
            pltpu.VMEM((PHASE_I * (tails + 3), span, channels), jnp.float32),
            pltpu.VMEM((PHASE_I * blocks, span, channels), jnp.float32),
        ]
        + masks
        + [pltpu.VMEM((PHASE_I, width, channels), jnp.float32)]
        + mats
        + [pltpu.SemaphoreType.DMA],
        compiler_params=pltpu.CompilerParams(vmem_limit_bytes=OUTER_MIB << 20),
        name="outer_blocks",
    )(wet, state, top, bottom, west, east, *bands, part, *weights)


def shift_pair(head, tail, axis):
    count = lax.axis_size(axis)
    before = lax.ppermute(tail, axis, [(i, (i + 1) % count) for i in range(count)])
    after = lax.ppermute(head, axis, [((i + 1) % count, i) for i in range(count)])
    return before, after


def per_device(
    ocean_field,
    wet_tiles,
    conv_weight,
    norm_gain,
    norm_bias,
    inner_weight,
    inner_bias,
    outer_weight,
    outer_bias,
):
    tile = ocean_field.shape[0] // wet_tiles.shape[0]
    cols = rim_cols_call(wet_tiles, ocean_field, tile)
    west, east = shift_pair(*cols, "lat")
    *rows, west, east = rim_rows_call(wet_tiles, ocean_field, west, east, tile)
    top, bottom = shift_pair(*rows, "lon")
    bands = []
    kernels = jnp.transpose(conv_weight, (1, 2, 0, 3))
    for layer in range(conv_weight.shape[0]):
        bands.append(band_call(kernels, layer))
    weights = (norm_gain, norm_bias, inner_weight, inner_bias, outer_weight, outer_bias)
    part = inner_call(wet_tiles, ocean_field, west, east, bands[0], weights, tile)
    return outer_call(wet_tiles, ocean_field, top, bottom, west, east, bands, part, weights, tile)


def solution(mesh):
    return jax.shard_map(
        per_device,
        mesh=mesh,
        in_specs=(P("lon", "lat", None), P("lon", "lat"), P(), P(), P(), P(), P(), P(), P()),
        out_specs=P("lon", "lat", None),
        check_vma=False,
    )
```
